32 devices in a mesh: dp: 8 (over z, x), tensor: 4 (over y, core).
Axes of the slice: x: 2, y: 2, z: 4, core: 2. Of those that a mesh axis runs over, the one named last changes fastest.
Arguments:
- tokens: bfloat16 [8192, 2048], P('dp'), may hold values from -6 to 6
- w_query: bfloat16 [2048, 2048], P('dp', 'tensor'), may hold values from -0.125 to 0.125
- w_key: bfloat16 [2048, 2048], P('dp', 'tensor'), may hold values from -0.125 to 0.125
- w_value: bfloat16 [2048, 4096], P('dp', 'tensor'), may hold values from -0.125 to 0.125
- w_gate: bfloat16 [2048, 4096], P('dp', 'tensor'), may hold values from -0.125 to 0.125
- w_out: bfloat16 [4096, 2048], P('tensor', 'dp'), may hold values from -0.125 to 0.125
- w_ffgate: bfloat16 [2048, 4096], P('dp', 'tensor'), may hold values from -0.125 to 0.125
- w_ffup: bfloat16 [2048, 4096], P('dp', 'tensor'), may hold values from -0.125 to 0.125
- w_down: bfloat16 [4096, 2048], P('tensor', 'dp'), may hold values from -0.125 to 0.125
- norm1_gain: bfloat16 [2048], P('dp'), may hold values from 0.5 to 1.5
- norm1_shift: bfloat16 [2048], P('dp'), may hold values from -1 to 1
- norm2_gain: bfloat16 [2048], P('dp'), may hold values from 0.5 to 1.5
- norm2_shift: bfloat16 [2048], P('dp'), may hold values from -1 to 1
- segment_ids: int32 [8192], P('dp'), may hold values from 0 to 63, never falling along the last dimension, each value on 1 to 512 neighbouring positions
- decay_index: int32 [8], P('tensor'), may hold values from 0 to 4
- cotangent: bfloat16 [8192, 2048], P('dp'), may hold values from -6 to 6
Outputs:
- block_out: bfloat16 [8192, 2048], P('dp')
- grad_tokens: float32 [8192, 2048], P('dp')
- grad_query: float32 [2048, 2048], P('dp', 'tensor')
- grad_key: float32 [2048, 2048], P('dp', 'tensor')
- grad_value: float32 [2048, 4096], P('dp', 'tensor')
- grad_gate: float32 [2048, 4096], P('dp', 'tensor')
- grad_out: float32 [4096, 2048], P('tensor', 'dp')
- grad_ffgate: float32 [2048, 4096], P('dp', 'tensor')
- grad_ffup: float32 [2048, 4096], P('dp', 'tensor')
- grad_down: float32 [4096, 2048], P('tensor', 'dp')
- grad_gain_one: float32 [2048], P('dp')
- grad_shift_one: float32 [2048], P('dp')
- grad_gain_two: float32 [2048], P('dp')
- grad_shift_two: float32 [2048], P('dp')
The draws below stay inside these ranges and needn't reach their ends.
Inputs may be any that keep to these rules, and one draw needn't show every extreme that they name: `segment_ids`: segment numbers never fall along the tokens; a sequence boundary resets retention even where the number continues.
All inputs are finite; a program needn't handle non-finite values.
Results may differ from the reference program's by a relative error of at most 0.018.
Values may be sent and summed in bfloat16 or wider, within the bound.
No kernel may reach another device: no remote copies, remote signals or barrier semaphores. Data moves between devices by JAX's collectives and lax.ppermute only.
A program may use at most 256 MiB of HBM per device.

```python
import math
import jax
import jax.numpy as jnp
import numpy as np
from jax import lax

D = 2048
HEADS = 8
HEAD_KEY = 256
HEAD_VALUE = 512
FF = 4096
LENGTH = 1024
TOKENS = 8192
QK = 2048
VW = 4096


def with_ends(array, key, low, high):
    longest = array.shape.index(max(array.shape))
    spots = []
    for shift in (0, 1):
        where = [jax.random.randint(jax.random.fold_in(key, axis), (), 0, length) for axis, length in enumerate(array.shape)]
        where[longest] = (where[longest] + shift) % array.shape[longest]
        spots.append(tuple(where))
    return array.at[spots[0]].set(low).at[spots[1]].set(high)


def levels(key, dims, cuts, low, largest):
    factor_of, own = 1.0, jax.random.fold_in(key, 6)
    for axis_at, shards_of in cuts:
        steps = jnp.exp(jax.random.uniform(jax.random.fold_in(own, axis_at), (shards_of,), jnp.float32, low / len(cuts), largest / len(cuts)))
        factor_of = factor_of * jnp.repeat(steps, dims[axis_at] // shards_of).reshape([-1 if axis == axis_at else 1 for axis in range(len(dims))])
    return factor_of


def length_profile(number_of, total, most, slope):
    loads = [(1 << 20) // math.isqrt(grade ** slope) + 1 for grade in range(2, number_of + 1)]
    spare, given = total - most - (number_of - 1), [1] * (number_of - 1)
    while spare > 0:
        candidates = [i for i in range(number_of - 1) if given[i] < most]
        mass, remaining = sum([loads[i] for i in candidates]), spare
        for i in candidates:
            addition = min(most - given[i], max(1, remaining * loads[i] // mass), spare)
            given[i] = given[i] + addition
            spare = spare - addition
    return np.array([most] + given)


def uneven(own_key, number_of, total, most, slope):
    if number_of == 2:
        one = jax.random.randint(own_key, (), max(1, total - most), min(most, total - 1) + 1)
        return jnp.stack([one, total - one])
    sizes = jnp.asarray(length_profile(number_of, total, most, slope), jnp.int32)
    couples = (number_of - 1) // 2
    source_of, receiver = sizes[1:1 + 2 * couples:2], sizes[2:2 + 2 * couples:2]
    margin = jnp.minimum(source_of - 1, most - receiver)
    shifted = jax.random.randint(jax.random.fold_in(own_key, 1), (couples,), 0, 1 << 20) % (margin + 1)
    sizes = sizes.at[1:1 + 2 * couples:2].set(source_of - shifted).at[2:2 + 2 * couples:2].set(receiver + shifted)
    return sizes[jax.random.permutation(jax.random.fold_in(own_key, 2), number_of)]


def bell_draw(stream_key, dims, scale, reach, cuts=(), kind=jnp.bfloat16):
    values = scale * jax.random.normal(stream_key, dims, jnp.float32)
    if cuts:
        values = values * levels(stream_key, dims, cuts, -0.22, 0.18)
    return jnp.clip(values, -reach, reach).astype(kind)


def setup_inputs(seed: int = 0) -> dict:
    splits = jax.random.split(jax.random.key(seed), 17)
    return {
        "tokens": bell_draw(splits[0], (TOKENS, D), 1.0, 6.0, ((0, 8),)),
        "w_query": bell_draw(splits[1], (D, QK), D ** -0.5, 0.125, ((0, 8), (1, 4))),
        "w_key": bell_draw(splits[2], (D, QK), D ** -0.5, 0.125, ((0, 8), (1, 4))),
        "w_value": bell_draw(splits[3], (D, VW), D ** -0.5, 0.125, ((0, 8), (1, 4))),
        "w_gate": bell_draw(splits[4], (D, VW), D ** -0.5, 0.125, ((0, 8), (1, 4))),
        "w_out": bell_draw(splits[5], (VW, D), (VW // 2) ** -0.5, 0.125, ((0, 4), (1, 8))),
        "w_ffgate": bell_draw(splits[6], (D, FF), D ** -0.5, 0.125, ((0, 8), (1, 4))),
        "w_ffup": bell_draw(splits[7], (D, FF), D ** -0.5, 0.125, ((0, 8), (1, 4))),
        "w_down": bell_draw(splits[8], (FF, D), (FF // 2) ** -0.5, 0.125, ((0, 4), (1, 8))),
        "norm1_gain": jnp.clip(1.0 + 0.1 * jax.random.normal(splits[9], (D,), jnp.float32), 0.5, 1.5).astype(jnp.bfloat16),
        "norm1_shift": bell_draw(splits[10], (D,), 0.2, 1.0, ((0, 8),)),
        "norm2_gain": jnp.clip(1.0 + 0.1 * jax.random.normal(splits[11], (D,), jnp.float32), 0.5, 1.5).astype(jnp.bfloat16),
        "norm2_shift": bell_draw(splits[12], (D,), 0.2, 1.0, ((0, 8),)),
        "segment_ids": jnp.searchsorted(jnp.cumsum(uneven(splits[13], TOKENS // (LENGTH // 8), TOKENS, LENGTH // 2, 2)), jnp.arange(TOKENS), side="right").astype(jnp.int32),
        "decay_index": with_ends(jax.random.randint(splits[14], (HEADS,), 0, 5), jax.random.fold_in(splits[14], 1), 0, 4).astype(jnp.int32),
        "cotangent": bell_draw(splits[15], (TOKENS, D), 1.0, 6.0, ((0, 8),)),
    }


@jax.custom_vjp
def low(v):
    return lax.optimization_barrier(v.astype(jnp.bfloat16)).astype(jnp.float32)

@jax.custom_vjp
def low_back(v):
    return v

def low_keep(v):
    return (low(v), None)

def low_pass(kept, grad):
    return (grad,)

def back_keep(v):
    return (v, None)

def back_low(kept, grad):
    return (low(grad),)
low.defvjp(low_keep, low_pass)
low_back.defvjp(back_keep, back_low)
EPSILON = 1e-05
GROUP_EPSILON = 1.0
XPOS_SPAN = 512.0
INV_ROOT2 = 1.0 / math.sqrt(2.0)
HIGHEST = lax.Precision.HIGHEST

def product(left, right):
    return jnp.dot(left, right, precision=HIGHEST, preferred_element_type=jnp.float32)

def layer_norm(values, gain, shift):
    centred = values - lax.optimization_barrier(jnp.mean(values, axis=-1, keepdims=True))
    variance = lax.optimization_barrier(jnp.mean(centred * centred, axis=-1, keepdims=True))
    return centred * lax.rsqrt(variance + EPSILON) * gain + shift

def xpos_tables(length, width):
    half = width // 2
    index = jnp.arange(half, dtype=jnp.float32)
    theta = jnp.exp(index * (-math.log(10000.0) / half))
    zeta = (2.0 * index + 0.4 * width) / (1.4 * width)
    position = jnp.arange(length, dtype=jnp.float32) - float(length // 2)
    angle = position[:, None] * theta[None, :]
    growth = jnp.exp(position[:, None] * (1.0 / XPOS_SPAN) * jnp.log(zeta)[None, :])
    return (jnp.cos(angle), jnp.sin(angle), growth)

def rotate(values, cosine, sine, factor):
    half = values.shape[-1] // 2
    first = values[..., :half]
    second = values[..., half:]
    cos_b = cosine[:, None, :]
    sin_b = sine[:, None, :]
    scale = factor[:, None, :]
    return jnp.concatenate([(first * cos_b - second * sin_b) * scale, (second * cos_b + first * sin_b) * scale], axis=-1)

def decay_mask(row_start, row_segment, col_segment, log_gamma):
    row_pos = row_start + jnp.arange(row_segment.shape[0], dtype=jnp.int32)
    col_pos = jnp.arange(col_segment.shape[0], dtype=jnp.int32)
    gap = row_pos[:, None] - col_pos[None, :]
    keep = (gap >= 0) & (row_segment[:, None] == col_segment[None, :])
    distance = jnp.maximum(gap, 0).astype(jnp.float32)
    return jnp.where(keep[None], jnp.exp(distance[None] * log_gamma[:, None, None]), 0.0)

def gelu(values):
    return values * (0.5 * (1.0 + lax.erf(values * INV_ROOT2)))

def block(weights, inputs, segment, log_gamma):
    w_query, w_key, w_value, w_gate, w_out, w_ffgate, w_ffup, w_down, gain_one, shift_one, gain_two, shift_two = weights
    length = inputs.shape[0]
    first_in = low(layer_norm(inputs, gain_one, shift_one))
    query = low_back(product(first_in, w_query)).reshape(length, HEADS, HEAD_KEY)
    keys = low_back(product(first_in, w_key)).reshape(length, HEADS, HEAD_KEY)
    values = low(low_back(product(first_in, w_value))).reshape(length, HEADS, HEAD_VALUE)
    gate = low_back(product(first_in, w_gate))
    cosine, sine, growth = xpos_tables(length, HEAD_KEY)
    query_rot = low(rotate(query, cosine, sine, growth))
    key_rot = low(rotate(keys, cosine, sine, 1.0 / growth) * HEAD_KEY ** (-0.5))
    raw = low_back(jnp.einsum('nhk,mhk->hnm', query_rot, key_rot, precision=HIGHEST))
    weighted = low(raw * decay_mask(0, segment, segment, log_gamma))
    mixed = low_back(jnp.einsum('hnm,mhv->nhv', weighted, values, precision=HIGHEST))
    centred = mixed - lax.optimization_barrier(jnp.mean(mixed, axis=-1, keepdims=True))
    grouped = centred * lax.rsqrt(lax.optimization_barrier(jnp.mean(centred * centred, axis=-1, keepdims=True)) + GROUP_EPSILON)
    grouped = grouped.reshape(length, HEADS * HEAD_VALUE)
    gated = low(jax.nn.silu(gate) * grouped)
    middle = inputs + low_back(product(gated, w_out))
    second_in = low(layer_norm(middle, gain_two, shift_two))
    ff_gate = low_back(product(second_in, w_ffgate))
    ff_up = low_back(product(second_in, w_ffup))
    hidden = low(gelu(ff_gate) * ff_up)
    return middle + low_back(product(hidden, w_down))

def reference(tokens, w_query, w_key, w_value, w_gate, w_out, w_ffgate, w_ffup, w_down, norm1_gain, norm1_shift, norm2_gain, norm2_shift, segment_ids, decay_index, cotangent):
    weights = tuple((item.astype(jnp.float32) for item in (w_query, w_key, w_value, w_gate, w_out, w_ffgate, w_ffup, w_down, norm1_gain, norm1_shift, norm2_gain, norm2_shift)))
    log_gamma = jnp.log1p(-jnp.exp2(-5.0 - decay_index.astype(jnp.float32)))
    seqs = tokens.shape[0] // LENGTH
    inputs = tokens.astype(jnp.float32).reshape(seqs, LENGTH, D)
    grads_in = cotangent.astype(jnp.float32).reshape(seqs, LENGTH, D)
    segments = segment_ids.reshape(seqs, LENGTH)

    def one_sequence(total, item):
        sequence, grad_seq, segment = item
        result, pull = jax.vjp(lambda params, values: block(params, values, segment, log_gamma), weights, sequence)
        grad_weights, grad_inputs = pull(grad_seq)
        return (jax.tree.map(jnp.add, total, grad_weights), (result, grad_inputs))
    zeros = jax.tree.map(jnp.zeros_like, weights)
    totals, (results, grad_inputs) = lax.scan(one_sequence, zeros, (inputs, grads_in, segments))
    block_out = results.reshape(seqs * LENGTH, D).astype(jnp.bfloat16)
    grad_tokens = grad_inputs.reshape(seqs * LENGTH, D)
    return (block_out, grad_tokens, totals[0], totals[1], totals[2], totals[3], totals[4], totals[5], totals[6], totals[7], totals[8], totals[9], totals[10], totals[11])
```

```python
import functools
import math

import jax
import jax.numpy as jnp
from jax import lax
from jax.sharding import PartitionSpec as P

HEAD_KEY = 256
HEAD_VALUE = 512
LENGTH = 1024


EPSILON = 1e-05
GROUP_EPSILON = 1.0
XPOS_SPAN = 512.0
INV_ROOT2 = 1.0 / math.sqrt(2.0)
INV_ROOT_TWO_PI = 1.0 / math.sqrt(2.0 * math.pi)

BOTH = ("dp", "tensor")


def xpos_tables(length, width):
    half = width // 2
    index = jnp.arange(half, dtype=jnp.float32)
    theta = jnp.exp(index * (-math.log(10000.0) / half))
    zeta = (2.0 * index + 0.4 * width) / (1.4 * width)
    position = jnp.arange(length, dtype=jnp.float32) - float(length // 2)
    angle = position[:, None] * theta[None, :]
    growth = jnp.exp(position[:, None] * (1.0 / XPOS_SPAN) * jnp.log(zeta)[None, :])
    return (jnp.cos(angle), jnp.sin(angle), growth)


def norm_parts(values, offset):
    centred = values - jnp.mean(values, axis=-1, keepdims=True)
    inv_scale = lax.rsqrt(jnp.mean(centred * centred, axis=-1, keepdims=True) + offset)
    return (centred * inv_scale, inv_scale)


def norm_back(grad_out, normed, inv_scale, gain):
    grad_norm = grad_out * gain
    return inv_scale * (
        grad_norm
        - jnp.mean(grad_norm, axis=-1, keepdims=True)
        - normed * jnp.mean(grad_norm * normed, axis=-1, keepdims=True)
    )


def dot_nn(left, right):
    return lax.dot_general(
        left, right, (((1,), (0,)), ((), ())), preferred_element_type=jnp.float32
    )


def dot_nt(left, right):
    return lax.dot_general(
        left, right, (((1,), (1,)), ((), ())), preferred_element_type=jnp.float32
    )


def dot_tn(left, right):
    return lax.dot_general(
        left, right, (((0,), (0,)), ((), ())), preferred_element_type=jnp.float32
    )


def together(*values):
    return lax.optimization_barrier(values)


def after(value, *others):
    return lax.optimization_barrier((value, *others))[0]


class Place:
    def __init__(self, ndp, nt):
        self.ndp, self.nt, self.na, self.ny = ndp, nt, ndp // 2, nt // 2
        index = lax.axis_index("dp")
        spot = lax.axis_index("tensor")
        self.a, self.b = index // 2, index % 2
        self.y, self.c = spot // 2, spot % 2
        self.keeper = self.b == self.c
        na, ny = self.na, self.ny
        self.ring = self.perm(lambda a, b, y, c: ((a + 1) % na, b, y, c))
        self.core = self.perm(lambda a, b, y, c: (a, b, y, 1 - c))
        self.across_x = self.perm(lambda a, b, y, c: (a, 1 - b, y, c))
        self.across_y = self.perm(lambda a, b, y, c: (a, b, 1 - y, c))
        self.across_both = self.perm(lambda a, b, y, c: (a, 1 - b, 1 - y, c))
        self.swap = self.perm(lambda a, b, y, c: (a, 1 - b, y, 1 - c) if b != c else None)
        self.home_x = self.perm(lambda a, b, y, c: (a, 1 - b, y, c) if b != c else None)
        self.home_y = self.perm(lambda a, b, y, c: (a, b, 1 - y, c) if b == c else None)
        self.home_core = self.perm(lambda a, b, y, c: (a, b, y, 1 - c) if b == c else None)
        self.group_ac = [
            [self.flat(a, b, y, c) for a in range(na) for c in range(2)]
            for b in range(2)
            for y in range(ny)
        ]
        self.group_a = [[2 * a + b for a in range(na)] for b in range(2)]

    def jump(self, step):
        return self.perm(lambda a, b, y, c: ((a + step) % self.na, b, y, c))

    def perm(self, move):
        pairs = []
        for a in range(self.na):
            for b in range(2):
                for y in range(self.ny):
                    for c in range(2):
                        to = move(a, b, y, c)
                        if to is not None:
                            pairs.append((self.flat(a, b, y, c), self.flat(*to)))
        return pairs

    def flat(self, a, b, y, c):
        return (2 * a + b) * self.nt + 2 * y + c


def send(value, pairs):
    return lax.ppermute(value, BOTH, pairs)


def rows_at(value, start, size):
    return lax.dynamic_slice_in_dim(value, start, size, axis=0)


def my_sequence(place, value):
    return jnp.where(place.keeper, value, send(value, place.swap))


def pick(keeper, value, received):
    return jnp.where(keeper, value, received)


def assemble(size, placed):
    first = placed[0][1]
    whole = jnp.zeros((size, *first.shape[1:]), first.dtype)
    for start, rows in placed:
        whole = lax.dynamic_update_slice_in_dim(whole, rows, start, axis=0)
    return whole


def row_starts(q, b, y):
    return (2 * y + b) * q, (4 + 2 * b + y) * q


def rows_of(value, b, y):
    q = value.shape[0] // 8
    first, second = row_starts(q, b, y)
    return rows_at(value, first, q), rows_at(value, second, q)


def my_rows(place, value):
    return jnp.concatenate(rows_of(value, place.b, place.y), axis=0)


def all_rows(place, pieces, others):
    width = pieces[0].shape[0]
    placed = []
    for j, (piece, other) in enumerate(zip(pieces, others)):
        at = 2 * ((place.a - j) % place.na)
        placed.append(((at + place.c) * width, piece))
        placed.append(((at + 1 - place.c) * width, other))
    return assemble(place.ndp * width, placed)


def queue_gather(place, own):
    return lax.all_gather(own, BOTH, axis=0, tiled=True, axis_index_groups=place.group_ac)


def core_halves(place, value):
    width = value.shape[1] // place.ndp

    def side(which):
        return jnp.concatenate(
            [
                lax.dynamic_slice_in_dim(value, (2 * j + which) * width, width, axis=1)
                for j in range(place.na)
            ],
            axis=1,
        )

    return side(place.c), side(1 - place.c)


def core_far(place, far, right):
    share = dot_tn(far, right).astype(jnp.bfloat16)
    return send(share, place.core), share


def core_near(near, right, got):
    return (dot_tn(near, right) + got.astype(jnp.float32)).astype(jnp.bfloat16)


def queue_scatter(place, value):
    return lax.psum_scatter(
        value, "dp", scatter_dimension=0, tiled=True, axis_index_groups=place.group_a
    )


def to_owner(place, value):
    return jnp.where(place.keeper, value, send(value, place.swap)).astype(jnp.float32)


def vector_grads(place, sums):
    parts = [send(sums, place.across_x), send(sums, place.across_y), send(sums, place.across_both)]
    sums = sums + parts[0] + (parts[1] + parts[2])
    sums = sums + send(sums, place.core)
    width = sums.shape[1] // place.ndp

    def block(a):
        return lax.dynamic_slice_in_dim(sums, (2 * a + place.b) * width, width, axis=1)

    total = block(place.a)
    for step in range(1, place.na):
        total = total + send(block((place.a + step) % place.na), place.jump(step))
    return total


def far_rows(place, value):
    y, b, q = place.y, place.b, value.shape[0] // 8
    return jnp.concatenate(
        [
            rows_at(value, (2 * (1 - y) + 1 - b) * q, q),
            rows_at(value, (2 * (1 - y) + b) * q, q),
            rows_at(value, (4 + 2 * (1 - b) + 1 - y) * q, q),
            rows_at(value, (4 + 2 * (1 - b) + y) * q, q),
        ],
        axis=0,
    )


def near_rows(place, value):
    y, b, q = place.y, place.b, value.shape[0] // 8
    return jnp.concatenate(
        [
            rows_at(value, (2 * y + 1 - b) * q, q),
            rows_at(value, (4 + 2 * b + 1 - y) * q, q),
            rows_at(value, (2 * y + b) * q, q),
            rows_at(value, (4 + 2 * b + y) * q, q),
        ],
        axis=0,
    )


def send_far(place, away):
    q = away.shape[0] // 4
    return (
        send(away[:q], place.across_y),
        send(away[2 * q : 3 * q], place.across_x),
        send(away[q : 2 * q], place.across_y),
        send(away[3 * q :], place.across_x),
    )


def sum_near(place, here, got):
    pass_a, pass_b, keep_a, keep_b = got
    q = pass_a.shape[0]
    share_a = (here[:q] + pass_a.astype(jnp.float32)).astype(jnp.bfloat16)
    share_b = (here[q : 2 * q] + pass_b.astype(jnp.float32)).astype(jnp.bfloat16)
    last_a = send(share_a, place.across_x)
    last_b = send(share_b, place.across_y)
    return (
        here[2 * q :]
        + jnp.concatenate([keep_a, keep_b], axis=0).astype(jnp.float32)
        + jnp.concatenate([last_a, last_b], axis=0).astype(jnp.float32)
    )


def gather_rows(place, own):
    q = own.shape[0] // 2
    y, b = place.y, place.b
    own_a, own_b = own[:q], own[q:]
    a_x = send(own_a, place.across_x)
    b_y = send(own_b, place.across_y)
    a_y = send(own_a, place.across_y)
    b_x = send(own_b, place.across_x)
    a_xy = send(a_x, place.across_y)
    b_xy = send(b_y, place.across_x)
    placed = []
    for first, second, bb, yy in (
        (own_a, own_b, b, y),
        (a_x, b_x, 1 - b, y),
        (a_y, b_y, b, 1 - y),
        (a_xy, b_xy, 1 - b, 1 - y),
    ):
        starts = row_starts(q, bb, yy)
        placed += [(starts[0], first), (starts[1], second)]
    return assemble(8 * q, placed)


def bring_home(place, own):
    q = own.shape[0] // 2
    y, b = place.y, place.b
    got = send(own, place.home_x)
    pieces = (
        (own, b, y),
        (got, 1 - b, y),
        (send(own, place.home_y), b, 1 - y),
        (send(got, place.home_y), 1 - b, 1 - y),
    )
    placed = []
    for rows, bb, yy in pieces:
        rows = jnp.where(place.keeper, rows, send(rows, place.home_core))
        starts = row_starts(q, bb, yy)
        placed += [(starts[0], rows[:q]), (starts[1], rows[q:])]
    return assemble(8 * q, placed)


def rotate(values, tables):
    cosine, sine, scale = tables
    half = values.shape[-1] // 2
    first, second = values[:, :half], values[:, half:]
    return jnp.concatenate(
        [(first * cosine - second * sine) * scale, (second * cosine + first * sine) * scale],
        axis=-1,
    )


def unrotate(grads, tables):
    cosine, sine, scale = tables
    half = grads.shape[-1] // 2
    first, second = grads[:, :half] * scale, grads[:, half:] * scale
    return jnp.concatenate(
        [first * cosine + second * sine, second * cosine - first * sine], axis=-1
    )


def decay_mask(row_start, row_segment, col_segment, log_gamma):
    row_pos = row_start + jnp.arange(row_segment.shape[0], dtype=jnp.int32)
    col_pos = jnp.arange(col_segment.shape[0], dtype=jnp.int32)
    gap = row_pos[:, None] - col_pos[None, :]
    keep = (gap >= 0) & (row_segment[:, None] == col_segment[None, :])
    distance = jnp.maximum(gap, 0).astype(jnp.float32)
    return jnp.where(keep, jnp.exp(distance * log_gamma), 0.0)


def retention_forward(query_rot, key_rot, values, segment, log_gamma):
    length = query_rot.shape[0]
    rows = min(512, length)
    outputs, kept = [], []
    for start in range(0, length, rows):
        stop = start + rows
        mask = decay_mask(start, segment[start:stop], segment[:stop], log_gamma)
        raw = dot_nt(query_rot[start:stop], key_rot[:stop])
        weighted = (raw * mask).astype(jnp.bfloat16)
        kept.append(weighted)
        outputs.append(dot_nn(weighted, values[:stop]))
    return jnp.concatenate(outputs, axis=0), kept


def retention_backward(query_rot, key_rot, values, segment, log_gamma, grad_mixed, kept):
    length = query_rot.shape[0]
    rows = min(512, length)
    grad_query, grad_key, grad_value = [], [], []
    for block, start in enumerate(range(0, length, rows)):
        stop = start + rows
        grad_block = grad_mixed[start:stop]
        mask = decay_mask(start, segment[start:stop], segment[:stop], log_gamma)
        grad_weighted = dot_nt(grad_block, values[:stop])
        grad_raw = (grad_weighted * mask).astype(jnp.bfloat16)
        grad_query.append(dot_nn(grad_raw, key_rot[:stop]))
        grad_key.append(dot_tn(grad_raw, query_rot[start:stop]))
        grad_value.append(dot_tn(kept[block], grad_block))

    def total(parts):
        out = []
        for start in range(0, length, rows):
            pieces = [p[start : start + rows] for p in parts if p.shape[0] > start]
            out.append(functools.reduce(jnp.add, pieces))
        return jnp.concatenate(out, axis=0)

    return jnp.concatenate(grad_query, axis=0), total(grad_key), total(grad_value)


def local(ndp, nt, *args):
    return layer(ndp, nt, *args)


def layer(
    ndp,
    nt,
    tokens,
    w_query,
    w_key,
    w_value,
    w_gate,
    w_out,
    w_ffgate,
    w_ffup,
    w_down,
    norm1_gain,
    norm1_shift,
    norm2_gain,
    norm2_shift,
    segment_ids,
    decay_index,
    cotangent,
):
    place = Place(ndp, nt)
    heads = w_query.shape[1] // HEAD_KEY
    split = heads * HEAD_KEY
    inner = heads * HEAD_VALUE
    units = w_ffgate.shape[1]

    width = norm1_gain.shape[0]
    norms = jnp.concatenate([norm1_gain, norm1_shift, norm2_gain, norm2_shift])
    across = w_value.shape[1]
    extra = -(-norms.shape[0] // across)
    norms = jnp.pad(norms, (0, 16 * across - norms.shape[0])).reshape(16, across)
    own_value = my_sequence(place, jnp.concatenate([w_value, norms], axis=0))
    own_qk = my_sequence(place, jnp.concatenate([w_query, w_key], axis=1))
    shard_og = jnp.concatenate([w_out.T, w_gate], axis=1)
    shard_ff = jnp.concatenate([w_ffgate, w_ffup], axis=1)
    shard_down = w_down.T
    got_tokens = send(tokens, place.swap)
    got_og = send(shard_og, place.swap)
    got_ff = send(shard_ff, place.swap)
    got_down = send(shard_down, place.swap)
    got_cotangent = send(cotangent, place.swap)
    value_pieces, qk_pieces = [own_value], [own_qk]
    for _ in range(1, place.na):
        value_pieces.append(send(value_pieces[-1], place.ring))
        qk_pieces.append(send(qk_pieces[-1], place.ring))
    value_others = [send(piece, place.core) for piece in value_pieces]
    qk_others = [send(piece, place.core) for piece in qk_pieces]
    norms = jnp.zeros((place.ndp, 4 * width), norms.dtype)
    for j in range(place.na):
        for piece, c in ((value_pieces[j], place.c), (value_others[j], 1 - place.c)):
            row = piece[width : width + extra].reshape(1, extra * across)[:, : 4 * width]
            at = 2 * ((place.a - j) % place.na) + c
            norms = lax.dynamic_update_slice_in_dim(norms, row, at, axis=0)
    norms = norms.reshape(place.ndp, 4, width).transpose(1, 0, 2).reshape(4, place.ndp * width)
    norms = norms.astype(jnp.float32)
    gain_one, shift_one, gain_two, shift_two = norms[0], norms[1], norms[2], norms[3]
    value_pieces = [piece[:width] for piece in value_pieces]
    value_others = [piece[:width] for piece in value_others]
    got_og, value_pieces[-2] = together(got_og, value_pieces[-2])
    got_tokens, qk_pieces[-2] = together(got_tokens, qk_pieces[-2])
    got_ff, got_down, value_pieces[-1] = together(got_ff, got_down, value_pieces[-1])
    own_og = pick(place.keeper, shard_og, got_og)
    own_ff = pick(place.keeper, shard_ff, got_ff)
    own_down = pick(place.keeper, shard_down, got_down)
    inputs = pick(place.keeper, tokens, got_tokens)
    full_value = all_rows(place, value_pieces, value_others)
    full_qk = all_rows(place, qk_pieces, qk_others)
    full_og = queue_gather(place, own_og)
    full_ff = queue_gather(place, own_ff)
    full_down = queue_gather(place, own_down)
    full_out, full_gate = full_og[:, :inner], full_og[:, inner:]
    segment = my_sequence(place, segment_ids)
    decay = jnp.where(place.keeper, decay_index, send(decay_index, place.core))
    log_gamma = jnp.log1p(-jnp.exp2(-5.0 - decay.astype(jnp.float32)))

    normed_all, _ = norm_parts(inputs.astype(jnp.float32), EPSILON)
    first_in = (normed_all * gain_one + shift_one).astype(jnp.bfloat16)
    qk = dot_nn(first_in, full_qk)
    values = dot_nn(first_in, full_value).astype(jnp.bfloat16)
    cosine, sine, growth = xpos_tables(LENGTH, HEAD_KEY)
    query_tables = (cosine, sine, growth)
    key_tables = (cosine, sine, 1.0 / growth)
    query_rot, key_rot = [], []
    for h in range(heads):
        query = qk[:, h * HEAD_KEY : (h + 1) * HEAD_KEY]
        keys = qk[:, split + h * HEAD_KEY : split + (h + 1) * HEAD_KEY]
        query_rot.append(rotate(query, query_tables).astype(jnp.bfloat16))
        key_rot.append((rotate(keys, key_tables) * HEAD_KEY ** (-0.5)).astype(jnp.bfloat16))
    grouped, group_scale, kept = [], [], []
    for h in range(heads):
        at = slice(h * HEAD_VALUE, (h + 1) * HEAD_VALUE)
        mixed, weighted = retention_forward(
            query_rot[h], key_rot[h], values[:, at], segment, log_gamma[h]
        )
        normed, scale = norm_parts(mixed, GROUP_EPSILON)
        grouped.append(normed)
        group_scale.append(scale)
        kept.append(weighted)
    grouped_flat = jnp.concatenate(grouped, axis=1)
    gate = dot_nn(first_in, full_gate)
    sigmoid_gate = jax.nn.sigmoid(gate)
    swish = gate * sigmoid_gate
    gated = (swish * grouped_flat).astype(jnp.bfloat16)
    got_cotangent, gated = together(got_cotangent, gated)
    grad_feed = pick(place.keeper, cotangent, got_cotangent)

    own_inputs = my_rows(place, inputs).astype(jnp.float32)
    away = dot_nt(far_rows(place, gated), full_out).astype(jnp.bfloat16)
    got = send_far(place, away)
    here = dot_nt(near_rows(place, after(gated, away)), full_out)
    middle = own_inputs + sum_near(place, here, got)
    normed_two, scale_two = norm_parts(middle, EPSILON)
    second_in = gather_rows(place, (normed_two * gain_two + shift_two).astype(jnp.bfloat16))

    ff_both = dot_nn(second_in, full_ff)
    ff_gate, ff_up = ff_both[:, :units], ff_both[:, units:]
    normal_cdf = 0.5 * (1.0 + lax.erf(ff_gate * INV_ROOT2))
    activation = ff_gate * normal_cdf
    hidden = (activation * ff_up).astype(jnp.bfloat16)
    feed_near, feed_far = core_halves(place, grad_feed)
    hidden, full_down = together(hidden, full_down)
    down_got, _ = core_far(place, feed_far, hidden)
    down_sum = core_near(feed_near, hidden, down_got)
    share_down = queue_scatter(place, down_sum)
    e_away = dot_nt(far_rows(place, hidden), full_down).astype(jnp.bfloat16)
    grad_hidden = dot_nn(grad_feed, full_down)
    density = jnp.exp(-0.5 * ff_gate * ff_gate) * INV_ROOT_TWO_PI
    grad_ff = jnp.concatenate(
        [
            (grad_hidden * ff_up * (normal_cdf + ff_gate * density)).astype(jnp.bfloat16),
            (grad_hidden * activation).astype(jnp.bfloat16),
        ],
        axis=1,
    )
    second_near, second_far = core_halves(place, second_in)
    ff_got, ff_far = core_far(place, second_far, grad_ff)
    away = dot_nt(far_rows(place, after(grad_ff, ff_far)), full_ff).astype(jnp.bfloat16)
    got = send_far(place, away)
    ff_sum = core_near(second_near, after(grad_ff, away), ff_got)
    ready, ff_sum = together(grad_ff, ff_sum)
    share_ff = queue_scatter(place, ff_sum)
    here = dot_nt(near_rows(place, ready), full_ff)
    grad_second = sum_near(place, here, got)
    grad_middle = my_rows(place, grad_feed).astype(jnp.float32) + norm_back(
        grad_second, normed_two, scale_two, gain_two
    )
    grad_branch = gather_rows(place, grad_middle.astype(jnp.bfloat16))
    e_got = send_far(place, e_away)
    branch_near, branch_far = core_halves(place, grad_branch)
    first_near, first_far = core_halves(place, first_in)
    out_got, out_far = core_far(place, branch_far, gated)
    grad_gated = dot_nn(after(grad_branch, out_far), full_out)
    swish_slope = sigmoid_gate * (1.0 + gate * (1.0 - sigmoid_gate))
    grad_gate_in = (grad_gated * grouped_flat * swish_slope).astype(jnp.bfloat16)
    grad_grouped = grad_gated * swish
    gate_got, gate_far = core_far(place, first_far, grad_gate_in)
    out_sum = core_near(branch_near, after(gated, gate_far), out_got)
    gate_sum = core_near(first_near, after(grad_gate_in, out_sum), gate_got)
    og_sum = jnp.concatenate([out_sum, gate_sum], axis=1)
    grad_grouped, og_sum, e_near = together(grad_grouped, og_sum, near_rows(place, hidden))
    share_og = queue_scatter(place, og_sum)
    here = dot_nt(e_near, full_down)
    feed = sum_near(place, here, e_got)
    block_out = bring_home(place, (middle + feed).astype(jnp.bfloat16))
    grad_qs, grad_ks, grad_vs = [], [], []
    for h in range(heads):
        at = slice(h * HEAD_VALUE, (h + 1) * HEAD_VALUE)
        grad_mixed = norm_back(grad_grouped[:, at], grouped[h], group_scale[h], 1.0).astype(
            jnp.bfloat16
        )
        grad_qrot, grad_krot, grad_value = retention_backward(
            query_rot[h], key_rot[h], values[:, at], segment, log_gamma[h], grad_mixed, kept[h]
        )
        grad_qs.append(unrotate(grad_qrot, query_tables).astype(jnp.bfloat16))
        grad_ks.append((unrotate(grad_krot, key_tables) * HEAD_KEY ** (-0.5)).astype(jnp.bfloat16))
        grad_vs.append(grad_value.astype(jnp.bfloat16))
    grad_vqk = jnp.concatenate(grad_vs + grad_qs + grad_ks, axis=1)

    def first_product(gate_rows, vqk_rows):
        return (
            dot_nt(gate_rows, full_gate)
            + dot_nt(vqk_rows[:, :inner], full_value)
            + dot_nt(vqk_rows[:, inner:], full_qk)
        )

    vqk_got, vqk_far = core_far(place, first_far, grad_vqk)
    ready = after(grad_vqk, vqk_far)
    away = first_product(far_rows(place, grad_gate_in), far_rows(place, ready)).astype(jnp.bfloat16)
    got = send_far(place, away)
    vqk_sum = core_near(first_near, after(grad_vqk, away), vqk_got)
    ready, vqk_sum = together(grad_vqk, vqk_sum)
    share_vqk = queue_scatter(place, vqk_sum)
    here = first_product(near_rows(place, grad_gate_in), near_rows(place, ready))
    grad_first = sum_near(place, here, got)
    normed_one, scale_one = norm_parts(own_inputs, EPSILON)
    grad_tokens = grad_middle + norm_back(grad_first, normed_one, scale_one, gain_one)
    grad_tokens = bring_home(place, grad_tokens.astype(jnp.bfloat16)).astype(jnp.float32)
    vectors = vector_grads(
        place,
        jnp.stack(
            [
                jnp.sum(grad_first * normed_one, axis=0),
                jnp.sum(grad_first, axis=0),
                jnp.sum(grad_second * normed_two, axis=0),
                jnp.sum(grad_second, axis=0),
            ]
        ),
    )
    share_down = to_owner(place, share_down).T
    share_ff = to_owner(place, share_ff)
    share_og = to_owner(place, share_og)
    share_vqk = to_owner(place, share_vqk)
    return (
        block_out,
        grad_tokens,
        share_vqk[:, inner : inner + split],
        share_vqk[:, inner + split :],
        share_vqk[:, :inner],
        share_og[:, inner:],
        share_og[:, :inner].T,
        share_ff[:, :units],
        share_ff[:, units:],
        share_down,
        vectors[0],
        vectors[1],
        vectors[2],
        vectors[3],
    )


def solution(mesh):
    placed = (
        P("dp", None),
        P("dp", "tensor"),
        P("dp", "tensor"),
        P("dp", "tensor"),
        P("dp", "tensor"),
        P("tensor", "dp"),
        P("dp", "tensor"),
        P("dp", "tensor"),
        P("tensor", "dp"),
        P("dp"),
        P("dp"),
        P("dp"),
        P("dp"),
        P("dp"),
        P("tensor"),
        P("dp", None),
    )
    return jax.shard_map(
        functools.partial(local, mesh.shape["dp"], mesh.shape["tensor"]),
        mesh=mesh,
        in_specs=placed,
        out_specs=(
            P("dp", None),
            P("dp", None),
            P("dp", "tensor"),
            P("dp", "tensor"),
            P("dp", "tensor"),
            P("dp", "tensor"),
            P("tensor", "dp"),
            P("dp", "tensor"),
            P("dp", "tensor"),
            P("tensor", "dp"),
            P("dp"),
            P("dp"),
            P("dp"),
            P("dp"),
        ),
        check_vma=False,
    )
```

```python
import functools
import math

import jax
import jax.numpy as jnp
from jax import lax
from jax.experimental import pallas as pl
from jax.experimental.pallas import tpu as pltpu
from jax.sharding import PartitionSpec as P

HEAD_KEY = 256
HEAD_VALUE = 512
LENGTH = 1024


EPSILON = 1e-05
GROUP_EPSILON = 1.0
XPOS_SPAN = 512.0
INV_ROOT2 = 1.0 / math.sqrt(2.0)
INV_ROOT_TWO_PI = 1.0 / math.sqrt(2.0 * math.pi)

BOTH = ("dp", "tensor")


def xpos_tables(length, width):
    half = width // 2
    index = jnp.arange(half, dtype=jnp.float32)
    theta = jnp.exp(index * (-math.log(10000.0) / half))
    zeta = (2.0 * index + 0.4 * width) / (1.4 * width)
    position = jnp.arange(length, dtype=jnp.float32) - float(length // 2)
    angle = position[:, None] * theta[None, :]
    growth = jnp.exp(position[:, None] * (1.0 / XPOS_SPAN) * jnp.log(zeta)[None, :])
    return (jnp.cos(angle), jnp.sin(angle), growth)


def norm_parts(values, offset):
    centred = values - jnp.mean(values, axis=-1, keepdims=True)
    inv_scale = lax.rsqrt(jnp.mean(centred * centred, axis=-1, keepdims=True) + offset)
    return (centred * inv_scale, inv_scale)


def norm_back(grad_out, normed, inv_scale, gain):
    grad_norm = grad_out * gain
    return inv_scale * (
        grad_norm
        - jnp.mean(grad_norm, axis=-1, keepdims=True)
        - normed * jnp.mean(grad_norm * normed, axis=-1, keepdims=True)
    )


def dot_nn(left, right):
    return lax.dot_general(
        left, right, (((1,), (0,)), ((), ())), preferred_element_type=jnp.float32
    )


def dot_nt(left, right):
    return lax.dot_general(
        left, right, (((1,), (1,)), ((), ())), preferred_element_type=jnp.float32
    )


def dot_tn(left, right):
    return lax.dot_general(
        left, right, (((0,), (0,)), ((), ())), preferred_element_type=jnp.float32
    )


def together(*values):
    return lax.optimization_barrier(values)


def after(value, *others):
    return lax.optimization_barrier((value, *others))[0]


class Place:
    def __init__(self, ndp, nt):
        self.ndp, self.nt, self.na, self.ny = ndp, nt, ndp // 2, nt // 2
        index = lax.axis_index("dp")
        spot = lax.axis_index("tensor")
        self.a, self.b = index // 2, index % 2
        self.y, self.c = spot // 2, spot % 2
        self.keeper = self.b == self.c
        na, ny = self.na, self.ny
        self.ring = self.perm(lambda a, b, y, c: ((a + 1) % na, b, y, c))
        self.core = self.perm(lambda a, b, y, c: (a, b, y, 1 - c))
        self.across_x = self.perm(lambda a, b, y, c: (a, 1 - b, y, c))
        self.across_y = self.perm(lambda a, b, y, c: (a, b, 1 - y, c))
        self.across_both = self.perm(lambda a, b, y, c: (a, 1 - b, 1 - y, c))
        self.swap = self.perm(lambda a, b, y, c: (a, 1 - b, y, 1 - c) if b != c else None)
        self.home_x = self.perm(lambda a, b, y, c: (a, 1 - b, y, c) if b != c else None)
        self.home_y = self.perm(lambda a, b, y, c: (a, b, 1 - y, c) if b == c else None)
        self.home_core = self.perm(lambda a, b, y, c: (a, b, y, 1 - c) if b == c else None)
        self.group_ac = [
            [self.flat(a, b, y, c) for a in range(na) for c in range(2)]
            for b in range(2)
            for y in range(ny)
        ]
        self.group_a = [[2 * a + b for a in range(na)] for b in range(2)]

    def jump(self, step):
        return self.perm(lambda a, b, y, c: ((a + step) % self.na, b, y, c))

    def perm(self, move):
        pairs = []
        for a in range(self.na):
            for b in range(2):
                for y in range(self.ny):
                    for c in range(2):
                        to = move(a, b, y, c)
                        if to is not None:
                            pairs.append((self.flat(a, b, y, c), self.flat(*to)))
        return pairs

    def flat(self, a, b, y, c):
        return (2 * a + b) * self.nt + 2 * y + c


def send(value, pairs):
    return lax.ppermute(value, BOTH, pairs)


def rows_at(value, start, size):
    return lax.dynamic_slice_in_dim(value, start, size, axis=0)


def my_sequence(place, value):
    return jnp.where(place.keeper, value, send(value, place.swap))


def pick(keeper, value, received):
    return jnp.where(keeper, value, received)


def assemble(size, placed):
    first = placed[0][1]
    whole = jnp.zeros((size, *first.shape[1:]), first.dtype)
    for start, rows in placed:
        whole = lax.dynamic_update_slice_in_dim(whole, rows, start, axis=0)
    return whole


def row_starts(q, b, y):
    return (2 * y + b) * q, (4 + 2 * b + y) * q


def rows_of(value, b, y):
    q = value.shape[0] // 8
    first, second = row_starts(q, b, y)
    return rows_at(value, first, q), rows_at(value, second, q)


def my_rows(place, value):
    return jnp.concatenate(rows_of(value, place.b, place.y), axis=0)


def queue_gather(place, own):
    return lax.all_gather(own, BOTH, axis=0, tiled=True, axis_index_groups=place.group_ac)


def core_halves(place, value):
    width = value.shape[1] // place.ndp

    def side(which):
        return jnp.concatenate(
            [
                lax.dynamic_slice_in_dim(value, (2 * j + which) * width, width, axis=1)
                for j in range(place.na)
            ],
            axis=1,
        )

    return side(place.c), side(1 - place.c)


def core_far(place, far, right):
    share = dot_tn(far, right).astype(jnp.bfloat16)
    return send(share, place.core), share


def core_near(near, right, got):
    return (dot_tn(near, right) + got.astype(jnp.float32)).astype(jnp.bfloat16)


def queue_scatter(place, value):
    return lax.psum_scatter(
        value, "dp", scatter_dimension=0, tiled=True, axis_index_groups=place.group_a
    )


def to_owner(place, value):
    return jnp.where(place.keeper, value, send(value, place.swap)).astype(jnp.float32)


def vector_grads(place, sums):
    ways = (place.across_x, place.across_y, place.across_both)
    parts = [send(sums, way) for way in ways]
    sums = sums + parts[0] + (parts[1] + parts[2])
    sums = sums + send(sums, place.core)
    width = sums.shape[1] // place.ndp

    def block(a):
        return lax.dynamic_slice_in_dim(sums, (2 * a + place.b) * width, width, axis=1)

    total = block(place.a)
    for step in range(1, place.na):
        total = total + send(block((place.a + step) % place.na), place.jump(step))
    return total


def far_rows(place, value):
    y, b, q = place.y, place.b, value.shape[0] // 8
    return jnp.concatenate(
        [
            rows_at(value, (2 * (1 - y) + 1 - b) * q, q),
            rows_at(value, (2 * (1 - y) + b) * q, q),
            rows_at(value, (4 + 2 * (1 - b) + 1 - y) * q, q),
            rows_at(value, (4 + 2 * (1 - b) + y) * q, q),
        ],
        axis=0,
    )


def near_rows(place, value):
    y, b, q = place.y, place.b, value.shape[0] // 8
    return jnp.concatenate(
        [
            rows_at(value, (2 * y + 1 - b) * q, q),
            rows_at(value, (4 + 2 * b + 1 - y) * q, q),
            rows_at(value, (2 * y + b) * q, q),
            rows_at(value, (4 + 2 * b + y) * q, q),
        ],
        axis=0,
    )


def send_far(place, away):
    q = away.shape[0] // 4
    return (
        send(away[:q], place.across_y),
        send(away[2 * q : 3 * q], place.across_x),
        send(away[q : 2 * q], place.across_y),
        send(away[3 * q :], place.across_x),
    )


def sum_near(place, here, got):
    pass_a, pass_b, keep_a, keep_b = got
    q = pass_a.shape[0]
    share_a = (here[:q] + pass_a.astype(jnp.float32)).astype(jnp.bfloat16)
    share_b = (here[q : 2 * q] + pass_b.astype(jnp.float32)).astype(jnp.bfloat16)
    last_a = send(share_a, place.across_x)
    last_b = send(share_b, place.across_y)
    return (
        here[2 * q :]
        + jnp.concatenate([keep_a, keep_b], axis=0).astype(jnp.float32)
        + jnp.concatenate([last_a, last_b], axis=0).astype(jnp.float32)
    )


def gather_rows(place, own):
    q = own.shape[0] // 2
    y, b = place.y, place.b
    own_a, own_b = own[:q], own[q:]
    a_x = send(own_a, place.across_x)
    b_y = send(own_b, place.across_y)
    a_y = send(own_a, place.across_y)
    b_x = send(own_b, place.across_x)
    a_xy = send(a_x, place.across_y)
    b_xy = send(b_y, place.across_x)
    placed = []
    for first, second, bb, yy in (
        (own_a, own_b, b, y),
        (a_x, b_x, 1 - b, y),
        (a_y, b_y, b, 1 - y),
        (a_xy, b_xy, 1 - b, 1 - y),
    ):
        starts = row_starts(q, bb, yy)
        placed += [(starts[0], first), (starts[1], second)]
    return assemble(8 * q, placed)


def bring_home(place, own):
    q = own.shape[0] // 2
    y, b = place.y, place.b
    got = send(own, place.home_x)
    pieces = (
        (own, b, y),
        (got, 1 - b, y),
        (send(own, place.home_y), b, 1 - y),
        (send(got, place.home_y), 1 - b, 1 - y),
    )
    placed = []
    for rows, bb, yy in pieces:
        rows = jnp.where(place.keeper, rows, send(rows, place.home_core))
        starts = row_starts(q, bb, yy)
        placed += [(starts[0], rows[:q]), (starts[1], rows[q:])]
    return assemble(8 * q, placed)


def decay_block(start, row_segment, col_segment, decay):
    shape = (row_segment.shape[0], col_segment.shape[1])
    gap = lax.broadcasted_iota(jnp.int32, shape, 0) - lax.broadcasted_iota(jnp.int32, shape, 1)
    gap = gap + start
    keep = (gap >= 0) & (row_segment == col_segment)
    distance = jnp.maximum(gap, 0).astype(jnp.float32)
    return jnp.where(keep, jnp.exp(distance * decay), 0.0)


def forward_kernel(head, na, given, *refs):
    log_gamma, row_segment, col_segment, cosine, sine, growth, tokens = refs[:7]
    pieces = refs[7 : 7 + 2 * na]
    full, parts, normed, scale, sems = refs[7 + 2 * na + given :]
    width = full.shape[0] // (2 * na)
    a, c = lax.axis_index("dp") // 2, lax.axis_index("tensor") % 2
    copies = []
    for j in range(na):
        for side in range(2):
            at = 2 * lax.rem(a - j + na, na) + (c if side == 0 else 1 - c)
            at = pl.ds(pl.multiple_of(at * width, width), width)
            piece = pieces[j + side * na].at[pl.ds(0, width), :]
            copies.append(pltpu.make_async_copy(piece, full.at[at, :], sems.at[2 * j + side]))
            copies[-1].start()
    for copy in copies:
        copy.wait()
    length = tokens.shape[0]
    rows = min(512, length)
    half = HEAD_KEY // 2

    def project(r, carry):
        at = pl.ds(pl.multiple_of(r * rows, rows), rows)
        left = tokens[at, :]
        for start in range(0, HEAD_VALUE, 256):
            stop = start + 256
            parts[at, start:stop] = dot_nn(left, full[:, start:stop]).astype(jnp.bfloat16)
        cos, sin, grow = cosine[at, :], sine[at, :], growth[at, :]
        for start, factor in (
            (HEAD_VALUE, grow),
            (HEAD_VALUE + HEAD_KEY, (1.0 / grow)),
        ):
            last = 1.0 if start == HEAD_VALUE else HEAD_KEY ** (-0.5)
            part = dot_nn(left, full[:, start : start + HEAD_KEY])
            first, second = part[:, :half], part[:, half:]
            parts[at, start : start + half] = (
                (first * cos - second * sin) * factor * last
            ).astype(jnp.bfloat16)
            parts[at, start + half : start + HEAD_KEY] = (
                (second * cos + first * sin) * factor * last
            ).astype(jnp.bfloat16)
        return carry

    lax.fori_loop(0, length // rows, project, 0)
    decay = log_gamma[head]
    query = slice(HEAD_VALUE, HEAD_VALUE + HEAD_KEY)
    key = slice(HEAD_VALUE + HEAD_KEY, HEAD_VALUE + 2 * HEAD_KEY)
    for i in range(length // rows):
        to = slice(i * rows, (i + 1) * rows)
        mixed = None
        for j in range(i + 1):
            of = slice(j * rows, (j + 1) * rows)
            mask = decay_block((i - j) * rows, row_segment[to, :], col_segment[:, of], decay)
            weighted = (dot_nt(parts[to, query], parts[of, key]) * mask).astype(jnp.bfloat16)
            part = dot_nn(weighted, parts[of, :HEAD_VALUE])
            mixed = part if mixed is None else mixed + part
        unit, inverse = norm_parts(mixed, GROUP_EPSILON)
        normed[to, :] = unit
        scale[to, :] = inverse


def retention_forward(place, head, shared, pieces, held):
    log_gamma, row_segment, col_segment, *tables, tokens = shared
    length, depth = tokens.shape
    heads = log_gamma.shape[0]
    width = HEAD_VALUE + 2 * HEAD_KEY
    anywhere = pl.BlockSpec(memory_space=pl.ANY)
    whole = lambda item: pl.BlockSpec(item.shape, lambda i: (0, 0))
    return pl.pallas_call(
        functools.partial(forward_kernel, head, place.na, len(held)),
        grid=(1,),
        in_specs=[
            pl.BlockSpec(memory_space=pltpu.SMEM),
            *[whole(item) for item in shared[1:]],
            *[anywhere] * (len(pieces) + len(held)),
        ],
        out_specs=[
            pl.BlockSpec((depth, width), lambda i: (0, 0)),
            pl.BlockSpec((length, width), lambda i: (0, head)),
            pl.BlockSpec((length, HEAD_VALUE), lambda i: (0, head)),
            pl.BlockSpec((None, length, 1), lambda i: (head, 0, 0)),
        ],
        out_shape=[
            jax.ShapeDtypeStruct((depth, width), jnp.bfloat16),
            jax.ShapeDtypeStruct((length, heads * width), jnp.bfloat16),
            jax.ShapeDtypeStruct((length, heads * HEAD_VALUE), jnp.float32),
            jax.ShapeDtypeStruct((heads, length, 1), jnp.float32),
        ],
        scratch_shapes=[pltpu.SemaphoreType.DMA((len(pieces),))],
        input_output_aliases={7 + len(pieces) + i: 1 + i for i in range(len(held))},
        compiler_params=pltpu.CompilerParams(vmem_limit_bytes=56 << 20),
        cost_estimate=pl.CostEstimate(
            flops=2 * length * (depth * width + length * (HEAD_KEY + HEAD_VALUE)),
            bytes_accessed=4 * length * width + 8 * depth * width,
            transcendentals=length * length,
        ),
    )(log_gamma, row_segment, col_segment, *tables, tokens, *pieces, *held)


def retention_kernel(
    log_gamma,
    row_segment,
    col_segment,
    cosine,
    sine,
    growth,
    value,
    query,
    key,
    grad,
    normed,
    scale,
    out,
    mixed,
    grad_query,
    grad_key,
    grad_value,
):
    length = query.shape[0]
    rows = min(512, length)
    decay = log_gamma[pl.program_id(0)]
    grads, unit = grad[...], normed[...]
    mixed[...] = (
        scale[...]
        * (
            grads
            - jnp.mean(grads, axis=-1, keepdims=True)
            - unit * jnp.mean(grads * unit, axis=-1, keepdims=True)
        )
    ).astype(jnp.bfloat16)
    for i in range(length // rows):
        to = slice(i * rows, (i + 1) * rows)
        for j in range(i + 1):
            of = slice(j * rows, (j + 1) * rows)
            mask = decay_block((i - j) * rows, row_segment[to, :], col_segment[:, of], decay)
            weighted = (dot_nt(query[to, :], key[of, :]) * mask).astype(jnp.bfloat16)
            raw = (dot_nt(mixed[to, :], value[of, :]) * mask).astype(jnp.bfloat16)
            parts = (
                (grad_query, to, dot_nn(raw, key[of, :]), j == 0),
                (grad_key, of, dot_tn(raw, query[to, :]), i == j),
                (grad_value, of, dot_tn(weighted, mixed[to, :]), i == j),
            )
            for total, at, part, first in parts:
                if first:
                    total[at, :] = part
                else:
                    total[at, :] += part
    cos, sin, grow = cosine[...], sine[...], growth[...]
    out[:, :HEAD_VALUE] = grad_value[...].astype(jnp.bfloat16)
    half = HEAD_KEY // 2
    for start, total, factor, last in (
        (HEAD_VALUE, grad_query, grow, 1.0),
        (HEAD_VALUE + HEAD_KEY, grad_key, 1.0 / grow, HEAD_KEY ** (-0.5)),
    ):
        first, second = total[:, :half] * factor, total[:, half:] * factor
        out[:, start : start + half] = ((first * cos + second * sin) * last).astype(jnp.bfloat16)
        out[:, start + half : start + HEAD_KEY] = ((second * cos - first * sin) * last).astype(
            jnp.bfloat16
        )


def retention_backward(
    log_gamma, row_segment, col_segment, cosine, sine, growth, vqk, grad, normed, scale
):
    length = vqk.shape[0]
    heads = log_gamma.shape[0]
    whole = lambda item: pl.BlockSpec(item.shape, lambda h: (0, 0))
    width = HEAD_VALUE + 2 * HEAD_KEY
    each, skip = width // HEAD_KEY, HEAD_VALUE // HEAD_KEY
    shared = (row_segment, col_segment, cosine, sine, growth)
    return pl.pallas_call(
        retention_kernel,
        grid=(heads,),
        in_specs=[
            pl.BlockSpec(memory_space=pltpu.SMEM),
            *[whole(item) for item in shared],
            pl.BlockSpec((length, HEAD_VALUE), lambda h: (0, h * (width // HEAD_VALUE))),
            pl.BlockSpec((length, HEAD_KEY), lambda h: (0, h * each + skip)),
            pl.BlockSpec((length, HEAD_KEY), lambda h: (0, h * each + skip + 1)),
            pl.BlockSpec((length, HEAD_VALUE), lambda h: (0, h)),
            pl.BlockSpec((length, HEAD_VALUE), lambda h: (0, h)),
            pl.BlockSpec((None, length, 1), lambda h: (h, 0, 0)),
        ],
        out_specs=pl.BlockSpec((length, width), lambda h: (0, h)),
        out_shape=jax.ShapeDtypeStruct((length, heads * width), jnp.bfloat16),
        scratch_shapes=[
            pltpu.VMEM((length, HEAD_VALUE), jnp.bfloat16),
            pltpu.VMEM((length, HEAD_KEY), jnp.float32),
            pltpu.VMEM((length, HEAD_KEY), jnp.float32),
            pltpu.VMEM((length, HEAD_VALUE), jnp.float32),
        ],
        compiler_params=pltpu.CompilerParams(vmem_limit_bytes=48 << 20),
        cost_estimate=pl.CostEstimate(
            flops=heads * length * length * 2 * (2 * HEAD_VALUE + 3 * HEAD_KEY),
            bytes_accessed=heads * length * (4 * width + 8 * HEAD_VALUE),
            transcendentals=heads * length * length,
        ),
    )(log_gamma, *shared, vqk, vqk, vqk, grad, normed, scale)


def local(ndp, nt, *args):
    return layer(ndp, nt, *args)


def layer(
    ndp,
    nt,
    tokens,
    w_query,
    w_key,
    w_value,
    w_gate,
    w_out,
    w_ffgate,
    w_ffup,
    w_down,
    norm1_gain,
    norm1_shift,
    norm2_gain,
    norm2_shift,
    segment_ids,
    decay_index,
    cotangent,
):
    place = Place(ndp, nt)
    heads = w_query.shape[1] // HEAD_KEY
    inner = heads * HEAD_VALUE
    units = w_ffgate.shape[1]

    width = norm1_gain.shape[0]
    norms = jnp.concatenate([norm1_gain, norm1_shift, norm2_gain, norm2_shift])
    across = w_value.shape[1]
    extra = -(-norms.shape[0] // across)
    norms = jnp.pad(norms, (0, 16 * across - norms.shape[0])).reshape(16, across)
    shards = [
        jnp.concatenate(
            [
                w_value[:, h * HEAD_VALUE : (h + 1) * HEAD_VALUE],
                w_query[:, h * HEAD_KEY : (h + 1) * HEAD_KEY],
                w_key[:, h * HEAD_KEY : (h + 1) * HEAD_KEY],
            ],
            axis=1,
        )
        for h in range(heads)
    ]
    own_value = my_sequence(place, jnp.concatenate([shards[0], norms], axis=0))
    own_qk = my_sequence(place, shards[1])
    shard_og = jnp.concatenate([w_out.T, w_gate], axis=1)
    shard_ff = jnp.concatenate([w_ffgate, w_ffup], axis=1)
    shard_down = w_down.T
    got_tokens = send(tokens, place.swap)
    got_og = send(shard_og, place.swap)
    got_ff = send(shard_ff, place.swap)
    got_down = send(shard_down, place.swap)
    got_cotangent = send(cotangent, place.swap)
    value_pieces, qk_pieces = [own_value], [own_qk]
    for _ in range(1, place.na):
        value_pieces.append(send(value_pieces[-1], place.ring))
        qk_pieces.append(send(qk_pieces[-1], place.ring))
    value_others = [send(piece, place.core) for piece in value_pieces]
    qk_others = [send(piece, place.core) for piece in qk_pieces]
    norms = jnp.zeros((place.ndp, 4 * width), norms.dtype)
    for j in range(place.na):
        for piece, c in ((value_pieces[j], place.c), (value_others[j], 1 - place.c)):
            row = piece[width : width + extra].reshape(1, extra * across)[:, : 4 * width]
            at = 2 * ((place.a - j) % place.na) + c
            norms = lax.dynamic_update_slice_in_dim(norms, row, at, axis=0)
    norms = norms.reshape(place.ndp, 4, width).transpose(1, 0, 2).reshape(4, place.ndp * width)
    norms = norms.astype(jnp.float32)
    gain_one, shift_one, gain_two, shift_two = norms[0], norms[1], norms[2], norms[3]
    got_og, value_pieces[-2] = together(got_og, value_pieces[-2])
    got_tokens, qk_pieces[-2] = together(got_tokens, qk_pieces[-2])
    own_og = pick(place.keeper, shard_og, got_og)
    inputs = pick(place.keeper, tokens, got_tokens)
    full_og = queue_gather(place, own_og)
    full_out, full_gate = full_og[:, :inner], full_og[:, inner:]
    segment = my_sequence(place, segment_ids)
    decay = jnp.where(place.keeper, decay_index, send(decay_index, place.core))
    log_gamma = jnp.log1p(-jnp.exp2(-5.0 - decay.astype(jnp.float32)))

    normed_all, _ = norm_parts(inputs.astype(jnp.float32), EPSILON)
    first_in = (normed_all * gain_one + shift_one).astype(jnp.bfloat16)
    tables = xpos_tables(LENGTH, HEAD_KEY)
    shared = (log_gamma, segment[:, None], segment[None, :], *tables, first_in)
    full_value, *held = retention_forward(place, 0, shared, value_pieces + value_others, ())
    full_qk, *held = retention_forward(place, 1, shared, qk_pieces + qk_others, held)
    vqk_rot, grouped_flat, group_scale = held
    got_ff, got_down, full_value = together(got_ff, got_down, full_value)
    full_ff = queue_gather(place, pick(place.keeper, shard_ff, got_ff))
    full_down = queue_gather(place, pick(place.keeper, shard_down, got_down))
    gate = dot_nn(first_in, full_gate)
    sigmoid_gate = jax.nn.sigmoid(gate)
    swish = gate * sigmoid_gate
    gated = (swish * grouped_flat).astype(jnp.bfloat16)
    got_cotangent, gated = together(got_cotangent, gated)
    grad_feed = pick(place.keeper, cotangent, got_cotangent)

    own_inputs = my_rows(place, inputs).astype(jnp.float32)
    away = dot_nt(far_rows(place, gated), full_out).astype(jnp.bfloat16)
    got = send_far(place, away)
    here = dot_nt(near_rows(place, after(gated, away)), full_out)
    middle = own_inputs + sum_near(place, here, got)
    normed_two, scale_two = norm_parts(middle, EPSILON)
    second_in = gather_rows(place, (normed_two * gain_two + shift_two).astype(jnp.bfloat16))

    ff_both = dot_nn(second_in, full_ff)
    ff_gate, ff_up = ff_both[:, :units], ff_both[:, units:]
    normal_cdf = 0.5 * (1.0 + lax.erf(ff_gate * INV_ROOT2))
    activation = ff_gate * normal_cdf
    hidden = (activation * ff_up).astype(jnp.bfloat16)
    feed_near, feed_far = core_halves(place, grad_feed)
    hidden, full_down = together(hidden, full_down)
    down_got, _ = core_far(place, feed_far, hidden)
    down_sum = core_near(feed_near, hidden, down_got)
    share_down = queue_scatter(place, down_sum)
    e_away = dot_nt(far_rows(place, hidden), full_down).astype(jnp.bfloat16)
    grad_hidden = dot_nn(grad_feed, full_down)
    density = jnp.exp(-0.5 * ff_gate * ff_gate) * INV_ROOT_TWO_PI
    grad_ff = jnp.concatenate(
        [
            (grad_hidden * ff_up * (normal_cdf + ff_gate * density)).astype(jnp.bfloat16),
            (grad_hidden * activation).astype(jnp.bfloat16),
        ],
        axis=1,
    )
    second_near, second_far = core_halves(place, second_in)
    away = dot_nt(far_rows(place, grad_ff), full_ff).astype(jnp.bfloat16)
    got = send_far(place, away)
    here = dot_nt(near_rows(place, after(grad_ff, away)), full_ff)
    ff_got, _ = core_far(place, second_far, after(grad_ff, here))
    ff_sum = core_near(second_near, grad_ff, ff_got)
    share_ff = queue_scatter(place, ff_sum)
    grad_second = sum_near(place, here, got)
    grad_middle = my_rows(place, grad_feed).astype(jnp.float32) + norm_back(
        grad_second, normed_two, scale_two, gain_two
    )
    grad_branch = gather_rows(place, grad_middle.astype(jnp.bfloat16))
    e_got = send_far(place, e_away)
    branch_near, branch_far = core_halves(place, grad_branch)
    first_near, first_far = core_halves(place, first_in)
    grad_gated = dot_nn(grad_branch, full_out)
    swish_slope = sigmoid_gate * (1.0 + gate * (1.0 - sigmoid_gate))
    grad_gate_in = (grad_gated * grouped_flat * swish_slope).astype(jnp.bfloat16)
    grad_grouped = grad_gated * swish
    gate_got, gate_far = core_far(place, first_far, grad_gate_in)
    out_got, out_far = core_far(place, branch_far, after(gated, gate_far))
    gate_sum = core_near(first_near, after(grad_gate_in, out_far), gate_got)
    out_sum = core_near(branch_near, after(gated, gate_sum), out_got)
    og_sum = jnp.concatenate([out_sum, gate_sum], axis=1)
    grad_grouped, og_sum, e_near = together(grad_grouped, og_sum, near_rows(place, hidden))
    share_og = queue_scatter(place, og_sum)
    here = dot_nt(e_near, full_down)
    feed = sum_near(place, here, e_got)
    block_out = bring_home(place, (middle + feed).astype(jnp.bfloat16))
    grad_vqk = retention_backward(*shared[:-1], vqk_rot, grad_grouped, grouped_flat, group_scale)

    def first_product(gate_rows, vqk_rows):
        return (
            dot_nt(gate_rows, full_gate)
            + dot_nt(vqk_rows[:, :inner], full_value)
            + dot_nt(vqk_rows[:, inner:], full_qk)
        )

    vqk_got, vqk_far = core_far(place, first_far, grad_vqk)
    ready = after(grad_vqk, vqk_far)
    away = first_product(far_rows(place, grad_gate_in), far_rows(place, ready)).astype(jnp.bfloat16)
    got = send_far(place, away)
    vqk_sum = core_near(first_near, after(grad_vqk, away), vqk_got)
    ready, vqk_sum = together(grad_vqk, vqk_sum)
    share_vqk = queue_scatter(place, vqk_sum)
    here = first_product(near_rows(place, grad_gate_in), near_rows(place, ready))
    grad_first = sum_near(place, here, got)
    normed_one, scale_one = norm_parts(own_inputs, EPSILON)
    grad_tokens = grad_middle + norm_back(grad_first, normed_one, scale_one, gain_one)
    grad_tokens = bring_home(place, grad_tokens.astype(jnp.bfloat16)).astype(jnp.float32)
    vectors = vector_grads(
        place,
        jnp.stack(
            [
                jnp.sum(grad_first * normed_one, axis=0),
                jnp.sum(grad_first, axis=0),
                jnp.sum(grad_second * normed_two, axis=0),
                jnp.sum(grad_second, axis=0),
            ]
        ),
    )
    share_down = to_owner(place, share_down).T
    share_ff = to_owner(place, share_ff)
    share_og = to_owner(place, share_og)
    share_vqk = to_owner(place, share_vqk)
    picks = []
    for start, size in ((HEAD_VALUE, HEAD_KEY), (HEAD_VALUE + HEAD_KEY, HEAD_KEY), (0, HEAD_VALUE)):
        each = HEAD_VALUE + 2 * HEAD_KEY
        picks.append(
            jnp.concatenate(
                [share_vqk[:, h * each + start : h * each + start + size] for h in range(heads)], axis=1
            )
        )
    return (
        block_out,
        grad_tokens,
        *picks,
        share_og[:, inner:],
        share_og[:, :inner].T,
        share_ff[:, :units],
        share_ff[:, units:],
        share_down,
        vectors[0],
        vectors[1],
        vectors[2],
        vectors[3],
    )


def solution(mesh):
    placed = (
        P("dp", None),
        P("dp", "tensor"),
        P("dp", "tensor"),
        P("dp", "tensor"),
        P("dp", "tensor"),
        P("tensor", "dp"),
        P("dp", "tensor"),
        P("dp", "tensor"),
        P("tensor", "dp"),
        P("dp"),
        P("dp"),
        P("dp"),
        P("dp"),
        P("dp"),
        P("tensor"),
        P("dp", None),
    )
    return jax.shard_map(
        functools.partial(local, mesh.shape["dp"], mesh.shape["tensor"]),
        mesh=mesh,
        in_specs=placed,
        out_specs=(
            P("dp", None),
            P("dp", None),
            P("dp", "tensor"),
            P("dp", "tensor"),
            P("dp", "tensor"),
            P("dp", "tensor"),
            P("tensor", "dp"),
            P("dp", "tensor"),
            P("dp", "tensor"),
            P("tensor", "dp"),
            P("dp"),
            P("dp"),
            P("dp"),
            P("dp"),
        ),
        check_vma=False,
    )
```

```python
import functools
import math

import jax
import jax.numpy as jnp
from jax import lax
from jax.experimental import pallas as pl
from jax.experimental.pallas import tpu as pltpu
from jax.sharding import PartitionSpec as P

HEAD_KEY = 256
HEAD_VALUE = 512
LENGTH = 1024


EPSILON = 1e-05
GROUP_EPSILON = 1.0
XPOS_SPAN = 512.0
INV_ROOT2 = 1.0 / math.sqrt(2.0)
INV_ROOT_TWO_PI = 1.0 / math.sqrt(2.0 * math.pi)

BOTH = ("dp", "tensor")


def xpos_tables(length, width):
    half = width // 2
    index = jnp.arange(half, dtype=jnp.float32)
    theta = jnp.exp(index * (-math.log(10000.0) / half))
    zeta = (2.0 * index + 0.4 * width) / (1.4 * width)
    position = jnp.arange(length, dtype=jnp.float32) - float(length // 2)
    angle = position[:, None] * theta[None, :]
    growth = jnp.exp(position[:, None] * (1.0 / XPOS_SPAN) * jnp.log(zeta)[None, :])
    return (jnp.cos(angle), jnp.sin(angle), growth)


def norm_parts(values, offset):
    centred = values - jnp.mean(values, axis=-1, keepdims=True)
    inv_scale = lax.rsqrt(jnp.mean(centred * centred, axis=-1, keepdims=True) + offset)
    return (centred * inv_scale, inv_scale)


def norm_back(grad_out, normed, inv_scale, gain):
    grad_norm = grad_out * gain
    return inv_scale * (
        grad_norm
        - jnp.mean(grad_norm, axis=-1, keepdims=True)
        - normed * jnp.mean(grad_norm * normed, axis=-1, keepdims=True)
    )


def dot_nn(left, right):
    return lax.dot_general(
        left, right, (((1,), (0,)), ((), ())), preferred_element_type=jnp.float32
    )


def dot_nt(left, right):
    return lax.dot_general(
        left, right, (((1,), (1,)), ((), ())), preferred_element_type=jnp.float32
    )


def dot_tn(left, right):
    return lax.dot_general(
        left, right, (((0,), (0,)), ((), ())), preferred_element_type=jnp.float32
    )


def together(*values):
    return lax.optimization_barrier(values)


def after(value, *others):
    return lax.optimization_barrier((value, *others))[0]


class Place:
    def __init__(self, ndp, nt):
        self.ndp, self.nt, self.na, self.ny = ndp, nt, ndp // 2, nt // 2
        index = lax.axis_index("dp")
        spot = lax.axis_index("tensor")
        self.a, self.b = index // 2, index % 2
        self.y, self.c = spot // 2, spot % 2
        self.keeper = self.b == self.c
        na, ny = self.na, self.ny
        self.ring = self.perm(lambda a, b, y, c: ((a + 1) % na, b, y, c))
        self.core = self.perm(lambda a, b, y, c: (a, b, y, 1 - c))
        self.across_x = self.perm(lambda a, b, y, c: (a, 1 - b, y, c))
        self.across_y = self.perm(lambda a, b, y, c: (a, b, 1 - y, c))
        self.across_both = self.perm(lambda a, b, y, c: (a, 1 - b, 1 - y, c))
        self.swap = self.perm(lambda a, b, y, c: (a, 1 - b, y, 1 - c) if b != c else None)
        self.home_x = self.perm(lambda a, b, y, c: (a, 1 - b, y, c) if b != c else None)
        self.home_y = self.perm(lambda a, b, y, c: (a, b, 1 - y, c) if b == c else None)
        self.home_core = self.perm(lambda a, b, y, c: (a, b, y, 1 - c) if b == c else None)
        self.group_ac = [
            [self.flat(a, b, y, c) for a in range(na) for c in range(2)]
            for b in range(2)
            for y in range(ny)
        ]
        self.group_a = [[2 * a + b for a in range(na)] for b in range(2)]

    def jump(self, step):
        return self.perm(lambda a, b, y, c: ((a + step) % self.na, b, y, c))

    def perm(self, move):
        pairs = []
        for a in range(self.na):
            for b in range(2):
                for y in range(self.ny):
                    for c in range(2):
                        to = move(a, b, y, c)
                        if to is not None:
                            pairs.append((self.flat(a, b, y, c), self.flat(*to)))
        return pairs

    def flat(self, a, b, y, c):
        return (2 * a + b) * self.nt + 2 * y + c


def send(value, pairs):
    return lax.ppermute(value, BOTH, pairs)


def rows_at(value, start, size):
    return lax.dynamic_slice_in_dim(value, start, size, axis=0)


def my_sequence(place, value):
    return jnp.where(place.keeper, value, send(value, place.swap))


def pick(keeper, value, received):
    return jnp.where(keeper, value, received)


def assemble(size, placed):
    first = placed[0][1]
    whole = jnp.zeros((size, *first.shape[1:]), first.dtype)
    for start, rows in placed:
        whole = lax.dynamic_update_slice_in_dim(whole, rows, start, axis=0)
    return whole


def row_starts(q, b, y):
    return (2 * y + b) * q, (4 + 2 * b + y) * q


def rows_of(value, b, y):
    q = value.shape[0] // 8
    first, second = row_starts(q, b, y)
    return rows_at(value, first, q), rows_at(value, second, q)


def my_rows(place, value):
    return jnp.concatenate(rows_of(value, place.b, place.y), axis=0)


def queue_gather(place, own):
    return lax.all_gather(own, BOTH, axis=0, tiled=True, axis_index_groups=place.group_ac)


def core_halves(place, value):
    width = value.shape[1] // place.ndp

    def side(which):
        return jnp.concatenate(
            [
                lax.dynamic_slice_in_dim(value, (2 * j + which) * width, width, axis=1)
                for j in range(place.na)
            ],
            axis=1,
        )

    return side(place.c), side(1 - place.c)


def core_far(place, far, right):
    share = dot_tn(far, right).astype(jnp.bfloat16)
    return send(share, place.core), share


def core_near(near, right, got):
    return (dot_tn(near, right) + got.astype(jnp.float32)).astype(jnp.bfloat16)


def queue_scatter(place, value):
    return lax.psum_scatter(
        value, "dp", scatter_dimension=0, tiled=True, axis_index_groups=place.group_a
    )


def to_owner(place, value):
    return jnp.where(place.keeper, value, send(value, place.swap)).astype(jnp.float32)


def vector_grads(place, sums):
    ways = (place.across_x, place.across_y, place.across_both)
    parts = [send(sums, way) for way in ways]
    sums = sums + parts[0] + (parts[1] + parts[2])
    sums = sums + send(sums, place.core)
    width = sums.shape[1] // place.ndp

    def block(a):
        return lax.dynamic_slice_in_dim(sums, (2 * a + place.b) * width, width, axis=1)

    total = block(place.a)
    for step in range(1, place.na):
        total = total + send(block((place.a + step) % place.na), place.jump(step))
    return total


def far_rows(place, value):
    y, b, q = place.y, place.b, value.shape[0] // 8
    return jnp.concatenate(
        [
            rows_at(value, (2 * (1 - y) + 1 - b) * q, q),
            rows_at(value, (2 * (1 - y) + b) * q, q),
            rows_at(value, (4 + 2 * (1 - b) + 1 - y) * q, q),
            rows_at(value, (4 + 2 * (1 - b) + y) * q, q),
        ],
        axis=0,
    )


def near_rows(place, value):
    y, b, q = place.y, place.b, value.shape[0] // 8
    return jnp.concatenate(
        [
            rows_at(value, (2 * y + 1 - b) * q, q),
            rows_at(value, (4 + 2 * b + 1 - y) * q, q),
            rows_at(value, (2 * y + b) * q, q),
            rows_at(value, (4 + 2 * b + y) * q, q),
        ],
        axis=0,
    )


def send_far(place, away):
    q = away.shape[0] // 4
    return (
        send(away[:q], place.across_y),
        send(away[2 * q : 3 * q], place.across_x),
        send(away[q : 2 * q], place.across_y),
        send(away[3 * q :], place.across_x),
    )


def sum_near(place, here, got):
    pass_a, pass_b, keep_a, keep_b = got
    q = pass_a.shape[0]
    share_a = (here[:q] + pass_a.astype(jnp.float32)).astype(jnp.bfloat16)
    share_b = (here[q : 2 * q] + pass_b.astype(jnp.float32)).astype(jnp.bfloat16)
    last_a = send(share_a, place.across_x)
    last_b = send(share_b, place.across_y)
    return (
        here[2 * q :]
        + jnp.concatenate([keep_a, keep_b], axis=0).astype(jnp.float32)
        + jnp.concatenate([last_a, last_b], axis=0).astype(jnp.float32)
    )


def gather_rows(place, own):
    q = own.shape[0] // 2
    y, b = place.y, place.b
    own_a, own_b = own[:q], own[q:]
    a_x = send(own_a, place.across_x)
    b_y = send(own_b, place.across_y)
    a_y = send(own_a, place.across_y)
    b_x = send(own_b, place.across_x)
    a_xy = send(a_x, place.across_y)
    b_xy = send(b_y, place.across_x)
    placed = []
    for first, second, bb, yy in (
        (own_a, own_b, b, y),
        (a_x, b_x, 1 - b, y),
        (a_y, b_y, b, 1 - y),
        (a_xy, b_xy, 1 - b, 1 - y),
    ):
        starts = row_starts(q, bb, yy)
        placed += [(starts[0], first), (starts[1], second)]
    return assemble(8 * q, placed)


def bring_home(place, own):
    q = own.shape[0] // 2
    y, b = place.y, place.b
    got = send(own, place.home_x)
    pieces = (
        (own, b, y),
        (got, 1 - b, y),
        (send(own, place.home_y), b, 1 - y),
        (send(got, place.home_y), 1 - b, 1 - y),
    )
    placed = []
    for rows, bb, yy in pieces:
        rows = jnp.where(place.keeper, rows, send(rows, place.home_core))
        starts = row_starts(q, bb, yy)
        placed += [(starts[0], rows[:q]), (starts[1], rows[q:])]
    return assemble(8 * q, placed)


def decay_block(start, row_segment, col_segment, decay):
    shape = (row_segment.shape[0], col_segment.shape[1])
    gap = lax.broadcasted_iota(jnp.int32, shape, 0) - lax.broadcasted_iota(jnp.int32, shape, 1)
    gap = gap + start
    keep = (gap >= 0) & (row_segment == col_segment)
    distance = jnp.maximum(gap, 0).astype(jnp.float32)
    return jnp.where(keep, jnp.exp(distance * decay), 0.0)


def forward_kernel(head, na, given, *refs):
    log_gamma, row_segment, col_segment, cosine, sine, growth, tokens = refs[:7]
    pieces = refs[7 : 7 + 2 * na]
    full, parts, normed, scale, sems = refs[7 + 2 * na + given :]
    width = full.shape[0] // (2 * na)
    a, c = lax.axis_index("dp") // 2, lax.axis_index("tensor") % 2
    copies = []
    for j in range(na):
        for side in range(2):
            at = 2 * lax.rem(a - j + na, na) + (c if side == 0 else 1 - c)
            at = pl.ds(pl.multiple_of(at * width, width), width)
            piece = pieces[j + side * na].at[pl.ds(0, width), :]
            copies.append(pltpu.make_async_copy(piece, full.at[at, :], sems.at[2 * j + side]))
            copies[-1].start()
    for copy in copies:
        copy.wait()
    length = tokens.shape[0]
    rows = min(512, length)
    half = HEAD_KEY // 2

    def project(r, carry):
        at = pl.ds(pl.multiple_of(r * rows, rows), rows)
        left = tokens[at, :]
        for start in range(0, HEAD_VALUE, 256):
            stop = start + 256
            parts[at, start:stop] = dot_nn(left, full[:, start:stop]).astype(jnp.bfloat16)
        cos, sin, grow = cosine[at, :], sine[at, :], growth[at, :]
        for start, factor in (
            (HEAD_VALUE, grow),
            (HEAD_VALUE + HEAD_KEY, (1.0 / grow)),
        ):
            last = 1.0 if start == HEAD_VALUE else HEAD_KEY ** (-0.5)
            part = dot_nn(left, full[:, start : start + HEAD_KEY])
            first, second = part[:, :half], part[:, half:]
            parts[at, start : start + half] = (
                (first * cos - second * sin) * factor * last
            ).astype(jnp.bfloat16)
            parts[at, start + half : start + HEAD_KEY] = (
                (second * cos + first * sin) * factor * last
            ).astype(jnp.bfloat16)
        return carry

    lax.fori_loop(0, length // rows, project, 0)
    decay = log_gamma[head]
    query = slice(HEAD_VALUE, HEAD_VALUE + HEAD_KEY)
    key = slice(HEAD_VALUE + HEAD_KEY, HEAD_VALUE + 2 * HEAD_KEY)
    for i in range(length // rows):
        to = slice(i * rows, (i + 1) * rows)
        mixed = None
        for j in range(i + 1):
            of = slice(j * rows, (j + 1) * rows)
            mask = decay_block((i - j) * rows, row_segment[to, :], col_segment[:, of], decay)
            weighted = (dot_nt(parts[to, query], parts[of, key]) * mask).astype(jnp.bfloat16)
            part = dot_nn(weighted, parts[of, :HEAD_VALUE])
            mixed = part if mixed is None else mixed + part
        unit, inverse = norm_parts(mixed, GROUP_EPSILON)
        normed[to, :] = unit
        scale[to, :] = inverse


def retention_forward(place, head, shared, pieces, held):
    log_gamma, row_segment, col_segment, *tables, tokens = shared
    length, depth = tokens.shape
    heads = log_gamma.shape[0]
    width = HEAD_VALUE + 2 * HEAD_KEY
    anywhere = pl.BlockSpec(memory_space=pl.ANY)
    whole = lambda item: pl.BlockSpec(item.shape, lambda i: (0, 0))
    return pl.pallas_call(
        functools.partial(forward_kernel, head, place.na, len(held)),
        grid=(1,),
        in_specs=[
            pl.BlockSpec(memory_space=pltpu.SMEM),
            *[whole(item) for item in shared[1:]],
            *[anywhere] * (len(pieces) + len(held)),
        ],
        out_specs=[
            pl.BlockSpec((depth, width), lambda i: (0, 0)),
            pl.BlockSpec((length, width), lambda i: (0, head)),
            pl.BlockSpec((length, HEAD_VALUE), lambda i: (0, head)),
            pl.BlockSpec((None, length, 1), lambda i: (head, 0, 0)),
        ],
        out_shape=[
            jax.ShapeDtypeStruct((depth, width), jnp.bfloat16),
            jax.ShapeDtypeStruct((length, heads * width), jnp.bfloat16),
            jax.ShapeDtypeStruct((length, heads * HEAD_VALUE), jnp.float32),
            jax.ShapeDtypeStruct((heads, length, 1), jnp.float32),
        ],
        scratch_shapes=[pltpu.SemaphoreType.DMA((len(pieces),))],
        input_output_aliases={7 + len(pieces) + i: 1 + i for i in range(len(held))},
        compiler_params=pltpu.CompilerParams(vmem_limit_bytes=56 << 20),
        cost_estimate=pl.CostEstimate(
            flops=2 * length * (depth * width + length * (HEAD_KEY + HEAD_VALUE)),
            bytes_accessed=4 * length * width + 8 * depth * width,
            transcendentals=length * length,
        ),
    )(log_gamma, row_segment, col_segment, *tables, tokens, *pieces, *held)


def retention_kernel(
    log_gamma,
    row_segment,
    col_segment,
    cosine,
    sine,
    growth,
    value,
    query,
    key,
    grad,
    normed,
    scale,
    out,
    mixed,
    grad_query,
    grad_key,
    grad_value,
):
    length = query.shape[0]
    rows = min(512, length)
    decay = log_gamma[pl.program_id(0)]
    grads, unit = grad[...], normed[...]
    mixed[...] = (
        scale[...]
        * (
            grads
            - jnp.mean(grads, axis=-1, keepdims=True)
            - unit * jnp.mean(grads * unit, axis=-1, keepdims=True)
        )
    ).astype(jnp.bfloat16)
    for i in range(length // rows):
        to = slice(i * rows, (i + 1) * rows)
        for j in range(i + 1):
            of = slice(j * rows, (j + 1) * rows)
            mask = decay_block((i - j) * rows, row_segment[to, :], col_segment[:, of], decay)
            weighted = (dot_nt(query[to, :], key[of, :]) * mask).astype(jnp.bfloat16)
            raw = (dot_nt(mixed[to, :], value[of, :]) * mask).astype(jnp.bfloat16)
            parts = (
                (grad_query, to, dot_nn(raw, key[of, :]), j == 0),
                (grad_key, of, dot_tn(raw, query[to, :]), i == j),
                (grad_value, of, dot_tn(weighted, mixed[to, :]), i == j),
            )
            for total, at, part, first in parts:
                if first:
                    total[at, :] = part
                else:
                    total[at, :] += part
    cos, sin, grow = cosine[...], sine[...], growth[...]
    out[:, :HEAD_VALUE] = grad_value[...].astype(jnp.bfloat16)
    half = HEAD_KEY // 2
    for start, total, factor, last in (
        (HEAD_VALUE, grad_query, grow, 1.0),
        (HEAD_VALUE + HEAD_KEY, grad_key, 1.0 / grow, HEAD_KEY ** (-0.5)),
    ):
        first, second = total[:, :half] * factor, total[:, half:] * factor
        out[:, start : start + half] = ((first * cos + second * sin) * last).astype(jnp.bfloat16)
        out[:, start + half : start + HEAD_KEY] = ((second * cos - first * sin) * last).astype(
            jnp.bfloat16
        )


def retention_backward(
    log_gamma, row_segment, col_segment, cosine, sine, growth, vqk, grad, normed, scale
):
    length = vqk.shape[0]
    heads = log_gamma.shape[0]
    whole = lambda item: pl.BlockSpec(item.shape, lambda h: (0, 0))
    width = HEAD_VALUE + 2 * HEAD_KEY
    each, skip = width // HEAD_KEY, HEAD_VALUE // HEAD_KEY
    shared = (row_segment, col_segment, cosine, sine, growth)
    return pl.pallas_call(
        retention_kernel,
        grid=(heads,),
        in_specs=[
            pl.BlockSpec(memory_space=pltpu.SMEM),
            *[whole(item) for item in shared],
            pl.BlockSpec((length, HEAD_VALUE), lambda h: (0, h * (width // HEAD_VALUE))),
            pl.BlockSpec((length, HEAD_KEY), lambda h: (0, h * each + skip)),
            pl.BlockSpec((length, HEAD_KEY), lambda h: (0, h * each + skip + 1)),
            pl.BlockSpec((length, HEAD_VALUE), lambda h: (0, h)),
            pl.BlockSpec((length, HEAD_VALUE), lambda h: (0, h)),
            pl.BlockSpec((None, length, 1), lambda h: (h, 0, 0)),
        ],
        out_specs=pl.BlockSpec((length, width), lambda h: (0, h)),
        out_shape=jax.ShapeDtypeStruct((length, heads * width), jnp.bfloat16),
        scratch_shapes=[
            pltpu.VMEM((length, HEAD_VALUE), jnp.bfloat16),
            pltpu.VMEM((length, HEAD_KEY), jnp.float32),
            pltpu.VMEM((length, HEAD_KEY), jnp.float32),
            pltpu.VMEM((length, HEAD_VALUE), jnp.float32),
        ],
        compiler_params=pltpu.CompilerParams(vmem_limit_bytes=48 << 20),
        cost_estimate=pl.CostEstimate(
            flops=heads * length * length * 2 * (2 * HEAD_VALUE + 3 * HEAD_KEY),
            bytes_accessed=heads * length * (4 * width + 8 * HEAD_VALUE),
            transcendentals=heads * length * length,
        ),
    )(log_gamma, *shared, vqk, vqk, vqk, grad, normed, scale)


def local(ndp, nt, *args):
    return layer(ndp, nt, *args)


def layer(
    ndp,
    nt,
    tokens,
    w_query,
    w_key,
    w_value,
    w_gate,
    w_out,
    w_ffgate,
    w_ffup,
    w_down,
    norm1_gain,
    norm1_shift,
    norm2_gain,
    norm2_shift,
    segment_ids,
    decay_index,
    cotangent,
):
    place = Place(ndp, nt)
    heads = w_query.shape[1] // HEAD_KEY
    inner = heads * HEAD_VALUE
    units = w_ffgate.shape[1]

    width = norm1_gain.shape[0]
    norms = jnp.concatenate([norm1_gain, norm1_shift, norm2_gain, norm2_shift])
    across = w_value.shape[1]
    extra = -(-norms.shape[0] // across)
    norms = jnp.pad(norms, (0, 16 * across - norms.shape[0])).reshape(16, across)
    shards = [
        jnp.concatenate(
            [
                w_value[:, h * HEAD_VALUE : (h + 1) * HEAD_VALUE],
                w_query[:, h * HEAD_KEY : (h + 1) * HEAD_KEY],
                w_key[:, h * HEAD_KEY : (h + 1) * HEAD_KEY],
            ],
            axis=1,
        )
        for h in range(heads)
    ]
    own_value = my_sequence(place, jnp.concatenate([shards[0], norms], axis=0))
    own_qk = my_sequence(place, shards[1])
    shard_og = jnp.concatenate([w_out.T, w_gate], axis=1)
    shard_ff = jnp.concatenate([w_ffgate, w_ffup], axis=1)
    shard_down = w_down.T
    got_tokens = send(tokens, place.swap)
    got_og = send(shard_og, place.swap)
    got_ff = send(shard_ff, place.swap)
    got_down = send(shard_down, place.swap)
    got_cotangent = send(cotangent, place.swap)
    value_pieces, qk_pieces = [own_value], [own_qk]
    for _ in range(1, place.na):
        value_pieces.append(send(value_pieces[-1], place.ring))
        qk_pieces.append(send(qk_pieces[-1], place.ring))
    value_others = [send(piece, place.core) for piece in value_pieces]
    qk_others = [send(piece, place.core) for piece in qk_pieces]
    norms = jnp.zeros((place.ndp, 4 * width), norms.dtype)
    for j in range(place.na):
        for piece, c in ((value_pieces[j], place.c), (value_others[j], 1 - place.c)):
            row = piece[width : width + extra].reshape(1, extra * across)[:, : 4 * width]
            at = 2 * ((place.a - j) % place.na) + c
            norms = lax.dynamic_update_slice_in_dim(norms, row, at, axis=0)
    norms = norms.reshape(place.ndp, 4, width).transpose(1, 0, 2).reshape(4, place.ndp * width)
    norms = norms.astype(jnp.float32)
    gain_one, shift_one, gain_two, shift_two = norms[0], norms[1], norms[2], norms[3]
    got_og, value_pieces[-2] = together(got_og, value_pieces[-2])
    got_tokens, qk_pieces[-2] = together(got_tokens, qk_pieces[-2])
    own_og = pick(place.keeper, shard_og, got_og)
    inputs = pick(place.keeper, tokens, got_tokens)
    full_og = queue_gather(place, own_og)
    full_out, full_gate = full_og[:, :inner], full_og[:, inner:]
    segment = my_sequence(place, segment_ids)
    decay = jnp.where(place.keeper, decay_index, send(decay_index, place.core))
    log_gamma = jnp.log1p(-jnp.exp2(-5.0 - decay.astype(jnp.float32)))

    normed_all, _ = norm_parts(inputs.astype(jnp.float32), EPSILON)
    first_in = (normed_all * gain_one + shift_one).astype(jnp.bfloat16)
    tables = xpos_tables(LENGTH, HEAD_KEY)
    shared = (log_gamma, segment[:, None], segment[None, :], *tables, first_in)
    full_value, *held = retention_forward(place, 0, shared, value_pieces + value_others, ())
    full_qk, *held = retention_forward(place, 1, shared, qk_pieces + qk_others, held)
    vqk_rot, grouped_flat, group_scale = held
    got_ff, got_down, full_value = together(got_ff, got_down, full_value)
    full_ff = queue_gather(place, pick(place.keeper, shard_ff, got_ff))
    full_down = queue_gather(place, pick(place.keeper, shard_down, got_down))
    gate = dot_nn(first_in, full_gate)
    sigmoid_gate = jax.nn.sigmoid(gate)
    swish = gate * sigmoid_gate
    gated = (swish * grouped_flat).astype(jnp.bfloat16)
    got_cotangent, gated = together(got_cotangent, gated)
    grad_feed = pick(place.keeper, cotangent, got_cotangent)

    own_inputs = my_rows(place, inputs).astype(jnp.float32)
    away = dot_nt(far_rows(place, gated), full_out).astype(jnp.bfloat16)
    got = send_far(place, away)
    here = dot_nt(near_rows(place, after(gated, away)), full_out)
    middle = own_inputs + sum_near(place, here, got)
    normed_two, scale_two = norm_parts(middle, EPSILON)
    second_in = gather_rows(place, (normed_two * gain_two + shift_two).astype(jnp.bfloat16))

    ff_both = dot_nn(second_in, full_ff)
    ff_gate, ff_up = ff_both[:, :units], ff_both[:, units:]
    hidden = (ff_gate * (0.5 * (1.0 + lax.erf(ff_gate * INV_ROOT2))) * ff_up).astype(jnp.bfloat16)
    hidden, ff_both = together(hidden, ff_both)
    feed_near, feed_far = core_halves(place, grad_feed)
    down_got, _ = core_far(place, feed_far, hidden)
    down_sum = core_near(feed_near, hidden, down_got)
    down_sum, full_down = together(down_sum, full_down)
    share_down = queue_scatter(place, down_sum)
    ff_gate, ff_up = ff_both[:, :units], ff_both[:, units:]
    normal_cdf = 0.5 * (1.0 + lax.erf(ff_gate * INV_ROOT2))
    activation = ff_gate * normal_cdf
    e_away = dot_nt(far_rows(place, hidden), full_down).astype(jnp.bfloat16)
    grad_hidden = dot_nn(grad_feed, full_down)
    density = jnp.exp(-0.5 * ff_gate * ff_gate) * INV_ROOT_TWO_PI
    grad_ff = jnp.concatenate(
        [
            (grad_hidden * ff_up * (normal_cdf + ff_gate * density)).astype(jnp.bfloat16),
            (grad_hidden * activation).astype(jnp.bfloat16),
        ],
        axis=1,
    )
    second_near, second_far = core_halves(place, second_in)
    away = dot_nt(far_rows(place, grad_ff), full_ff).astype(jnp.bfloat16)
    got = send_far(place, away)
    here = dot_nt(near_rows(place, after(grad_ff, away)), full_ff)
    ff_got, _ = core_far(place, second_far, after(grad_ff, here))
    ff_sum = core_near(second_near, grad_ff, ff_got)
    share_ff = queue_scatter(place, ff_sum)
    grad_second = sum_near(place, here, got)
    grad_middle = my_rows(place, grad_feed).astype(jnp.float32) + norm_back(
        grad_second, normed_two, scale_two, gain_two
    )
    grad_branch = gather_rows(place, grad_middle.astype(jnp.bfloat16))
    e_got = send_far(place, e_away)
    branch_near, branch_far = core_halves(place, grad_branch)
    first_near, first_far = core_halves(place, first_in)
    grad_gated = dot_nn(grad_branch, full_out)
    swish_slope = sigmoid_gate * (1.0 + gate * (1.0 - sigmoid_gate))
    grad_gate_in = (grad_gated * grouped_flat * swish_slope).astype(jnp.bfloat16)
    grad_grouped = grad_gated * swish
    gate_got, gate_far = core_far(place, first_far, grad_gate_in)
    out_got, out_far = core_far(place, branch_far, after(gated, gate_far))
    gate_sum = core_near(first_near, after(grad_gate_in, out_far), gate_got)
    out_sum = core_near(branch_near, after(gated, gate_sum), out_got)
    og_sum = jnp.concatenate([out_sum, gate_sum], axis=1)
    grad_grouped, og_sum, e_near = together(grad_grouped, og_sum, near_rows(place, hidden))
    share_og = queue_scatter(place, og_sum)
    here = dot_nt(e_near, full_down)
    feed = sum_near(place, here, e_got)
    block_out = bring_home(place, (middle + feed).astype(jnp.bfloat16))
    grad_vqk = retention_backward(*shared[:-1], vqk_rot, grad_grouped, grouped_flat, group_scale)

    def first_product(gate_rows, vqk_rows):
        return (
            dot_nt(gate_rows, full_gate)
            + dot_nt(vqk_rows[:, :inner], full_value)
            + dot_nt(vqk_rows[:, inner:], full_qk)
        )

    vqk_got, vqk_far = core_far(place, first_far, grad_vqk)
    ready = after(grad_vqk, vqk_far)
    away = first_product(far_rows(place, grad_gate_in), far_rows(place, ready)).astype(jnp.bfloat16)
    got = send_far(place, away)
    vqk_sum = core_near(first_near, after(grad_vqk, away), vqk_got)
    ready, vqk_sum = together(grad_vqk, vqk_sum)
    share_vqk = queue_scatter(place, vqk_sum)
    here = first_product(near_rows(place, grad_gate_in), near_rows(place, ready))
    grad_first = sum_near(place, here, got)
    normed_one, scale_one = norm_parts(own_inputs, EPSILON)
    grad_tokens = grad_middle + norm_back(grad_first, normed_one, scale_one, gain_one)
    grad_tokens = bring_home(place, grad_tokens.astype(jnp.bfloat16)).astype(jnp.float32)
    vectors = vector_grads(
        place,
        jnp.stack(
            [
                jnp.sum(grad_first * normed_one, axis=0),
                jnp.sum(grad_first, axis=0),
                jnp.sum(grad_second * normed_two, axis=0),
                jnp.sum(grad_second, axis=0),
            ]
        ),
    )
    share_down = to_owner(place, share_down).T
    share_ff = to_owner(place, share_ff)
    share_og = to_owner(place, share_og)
    share_vqk, grad_tokens = together(share_vqk, grad_tokens)
    share_vqk = to_owner(place, share_vqk)
    picks = []
    for start, size in ((HEAD_VALUE, HEAD_KEY), (HEAD_VALUE + HEAD_KEY, HEAD_KEY), (0, HEAD_VALUE)):
        each = HEAD_VALUE + 2 * HEAD_KEY
        picks.append(
            jnp.concatenate(
                [share_vqk[:, h * each + start : h * each + start + size] for h in range(heads)], axis=1
            )
        )
    return (
        block_out,
        grad_tokens,
        *picks,
        share_og[:, inner:],
        share_og[:, :inner].T,
        share_ff[:, :units],
        share_ff[:, units:],
        share_down,
        vectors[0],
        vectors[1],
        vectors[2],
        vectors[3],
    )


def solution(mesh):
    placed = (
        P("dp", None),
        P("dp", "tensor"),
        P("dp", "tensor"),
        P("dp", "tensor"),
        P("dp", "tensor"),
        P("tensor", "dp"),
        P("dp", "tensor"),
        P("dp", "tensor"),
        P("tensor", "dp"),
        P("dp"),
        P("dp"),
        P("dp"),
        P("dp"),
        P("dp"),
        P("tensor"),
        P("dp", None),
    )
    return jax.shard_map(
        functools.partial(local, mesh.shape["dp"], mesh.shape["tensor"]),
        mesh=mesh,
        in_specs=placed,
        out_specs=(
            P("dp", None),
            P("dp", None),
            P("dp", "tensor"),
            P("dp", "tensor"),
            P("dp", "tensor"),
            P("dp", "tensor"),
            P("tensor", "dp"),
            P("dp", "tensor"),
            P("dp", "tensor"),
            P("tensor", "dp"),
            P("dp"),
            P("dp"),
            P("dp"),
            P("dp"),
        ),
        check_vma=False,
    )
```

```python
import functools
import math

import jax
import jax.numpy as jnp
from jax import lax
from jax.experimental import pallas as pl
from jax.experimental.pallas import tpu as pltpu
from jax.sharding import PartitionSpec as P

HEAD_KEY = 256
HEAD_VALUE = 512
LENGTH = 1024


EPSILON = 1e-05
GROUP_EPSILON = 1.0
XPOS_SPAN = 512.0
INV_ROOT2 = 1.0 / math.sqrt(2.0)
INV_ROOT_TWO_PI = 1.0 / math.sqrt(2.0 * math.pi)

BOTH = ("dp", "tensor")


def xpos_tables(length, width):
    half = width // 2
    index = jnp.arange(half, dtype=jnp.float32)
    theta = jnp.exp(index * (-math.log(10000.0) / half))
    zeta = (2.0 * index + 0.4 * width) / (1.4 * width)
    position = jnp.arange(length, dtype=jnp.float32) - float(length // 2)
    angle = position[:, None] * theta[None, :]
    growth = jnp.exp(position[:, None] * (1.0 / XPOS_SPAN) * jnp.log(zeta)[None, :])
    return (jnp.cos(angle), jnp.sin(angle), growth)


def norm_parts(values, offset):
    centred = values - jnp.mean(values, axis=-1, keepdims=True)
    inv_scale = lax.rsqrt(jnp.mean(centred * centred, axis=-1, keepdims=True) + offset)
    return (centred * inv_scale, inv_scale)


def norm_back(grad_out, normed, inv_scale, gain):
    grad_norm = grad_out * gain
    return inv_scale * (
        grad_norm
        - jnp.mean(grad_norm, axis=-1, keepdims=True)
        - normed * jnp.mean(grad_norm * normed, axis=-1, keepdims=True)
    )


def dot_nn(left, right):
    return lax.dot_general(
        left, right, (((1,), (0,)), ((), ())), preferred_element_type=jnp.float32
    )


def dot_nt(left, right):
    return lax.dot_general(
        left, right, (((1,), (1,)), ((), ())), preferred_element_type=jnp.float32
    )


def dot_tn(left, right):
    return lax.dot_general(
        left, right, (((0,), (0,)), ((), ())), preferred_element_type=jnp.float32
    )


def together(*values):
    return lax.optimization_barrier(values)


def after(value, *others):
    return lax.optimization_barrier((value, *others))[0]


class Place:
    def __init__(self, ndp, nt):
        self.ndp, self.nt, self.na, self.ny = ndp, nt, ndp // 2, nt // 2
        index = lax.axis_index("dp")
        spot = lax.axis_index("tensor")
        self.a, self.b = index // 2, index % 2
        self.y, self.c = spot // 2, spot % 2
        self.keeper = self.b == self.c
        na, ny = self.na, self.ny
        self.ring = self.perm(lambda a, b, y, c: ((a + 1) % na, b, y, c))
        self.core = self.perm(lambda a, b, y, c: (a, b, y, 1 - c))
        self.across_x = self.perm(lambda a, b, y, c: (a, 1 - b, y, c))
        self.across_y = self.perm(lambda a, b, y, c: (a, b, 1 - y, c))
        self.across_both = self.perm(lambda a, b, y, c: (a, 1 - b, 1 - y, c))
        self.swap = self.perm(lambda a, b, y, c: (a, 1 - b, y, 1 - c) if b != c else None)
        self.home_x = self.perm(lambda a, b, y, c: (a, 1 - b, y, c) if b != c else None)
        self.home_y = self.perm(lambda a, b, y, c: (a, b, 1 - y, c) if b == c else None)
        self.home_core = self.perm(lambda a, b, y, c: (a, b, y, 1 - c) if b == c else None)
        self.group_ac = [
            [self.flat(a, b, y, c) for a in range(na) for c in range(2)]
            for b in range(2)
            for y in range(ny)
        ]
        self.group_a = [[2 * a + b for a in range(na)] for b in range(2)]

    def jump(self, step):
        return self.perm(lambda a, b, y, c: ((a + step) % self.na, b, y, c))

    def perm(self, move):
        pairs = []
        for a in range(self.na):
            for b in range(2):
                for y in range(self.ny):
                    for c in range(2):
                        to = move(a, b, y, c)
                        if to is not None:
                            pairs.append((self.flat(a, b, y, c), self.flat(*to)))
        return pairs

    def flat(self, a, b, y, c):
        return (2 * a + b) * self.nt + 2 * y + c


def send(value, pairs):
    return lax.ppermute(value, BOTH, pairs)


def rows_at(value, start, size):
    return lax.dynamic_slice_in_dim(value, start, size, axis=0)


def my_sequence(place, value):
    return jnp.where(place.keeper, value, send(value, place.swap))


def pick(keeper, value, received):
    return jnp.where(keeper, value, received)


def assemble(size, placed):
    first = placed[0][1]
    whole = jnp.zeros((size, *first.shape[1:]), first.dtype)
    for start, rows in placed:
        whole = lax.dynamic_update_slice_in_dim(whole, rows, start, axis=0)
    return whole


def row_starts(q, b, y):
    return (2 * y + b) * q, (4 + 2 * b + y) * q


def rows_of(value, b, y):
    q = value.shape[0] // 8
    first, second = row_starts(q, b, y)
    return rows_at(value, first, q), rows_at(value, second, q)


def my_rows(place, value):
    return jnp.concatenate(rows_of(value, place.b, place.y), axis=0)


def queue_gather(place, own):
    return lax.all_gather(own, BOTH, axis=0, tiled=True, axis_index_groups=place.group_ac)


def core_halves(place, value):
    width = value.shape[1] // place.ndp

    def side(which):
        return jnp.concatenate(
            [
                lax.dynamic_slice_in_dim(value, (2 * j + which) * width, width, axis=1)
                for j in range(place.na)
            ],
            axis=1,
        )

    return side(place.c), side(1 - place.c)


def core_far(place, far, right):
    share = dot_tn(far, right).astype(jnp.bfloat16)
    return send(share, place.core), share


def core_near(near, right, got):
    return (dot_tn(near, right) + got.astype(jnp.float32)).astype(jnp.bfloat16)


def queue_scatter(place, value):
    return lax.psum_scatter(
        value, "dp", scatter_dimension=0, tiled=True, axis_index_groups=place.group_a
    )


def to_owner(place, value):
    return jnp.where(place.keeper, value, send(value, place.swap)).astype(jnp.float32)


def vector_grads(place, sums):
    ways = (place.across_x, place.across_y, place.across_both)
    parts = [send(sums, way) for way in ways]
    sums = sums + parts[0] + (parts[1] + parts[2])
    sums = sums + send(sums, place.core)
    width = sums.shape[1] // place.ndp

    def block(a):
        return lax.dynamic_slice_in_dim(sums, (2 * a + place.b) * width, width, axis=1)

    total = block(place.a)
    for step in range(1, place.na):
        total = total + send(block((place.a + step) % place.na), place.jump(step))
    return total


def far_rows(place, value):
    y, b, q = place.y, place.b, value.shape[0] // 8
    return jnp.concatenate(
        [
            rows_at(value, (2 * (1 - y) + 1 - b) * q, q),
            rows_at(value, (2 * (1 - y) + b) * q, q),
            rows_at(value, (4 + 2 * (1 - b) + 1 - y) * q, q),
            rows_at(value, (4 + 2 * (1 - b) + y) * q, q),
        ],
        axis=0,
    )


def near_rows(place, value):
    y, b, q = place.y, place.b, value.shape[0] // 8
    return jnp.concatenate(
        [
            rows_at(value, (2 * y + 1 - b) * q, q),
            rows_at(value, (4 + 2 * b + 1 - y) * q, q),
            rows_at(value, (2 * y + b) * q, q),
            rows_at(value, (4 + 2 * b + y) * q, q),
        ],
        axis=0,
    )


def send_far(place, away):
    q = away.shape[0] // 4
    return (
        send(away[:q], place.across_y),
        send(away[2 * q : 3 * q], place.across_x),
        send(away[q : 2 * q], place.across_y),
        send(away[3 * q :], place.across_x),
    )


def sum_near(place, here, got):
    pass_a, pass_b, keep_a, keep_b = got
    q = pass_a.shape[0]
    share_a = (here[:q] + pass_a.astype(jnp.float32)).astype(jnp.bfloat16)
    share_b = (here[q : 2 * q] + pass_b.astype(jnp.float32)).astype(jnp.bfloat16)
    last_a = send(share_a, place.across_x)
    last_b = send(share_b, place.across_y)
    return (
        here[2 * q :]
        + jnp.concatenate([keep_a, keep_b], axis=0).astype(jnp.float32)
        + jnp.concatenate([last_a, last_b], axis=0).astype(jnp.float32)
    )


def gather_rows(place, own):
    q = own.shape[0] // 2
    y, b = place.y, place.b
    own_a, own_b = own[:q], own[q:]
    a_x = send(own_a, place.across_x)
    b_y = send(own_b, place.across_y)
    a_y = send(own_a, place.across_y)
    b_x = send(own_b, place.across_x)
    a_xy = send(a_x, place.across_y)
    b_xy = send(b_y, place.across_x)
    placed = []
    for first, second, bb, yy in (
        (own_a, own_b, b, y),
        (a_x, b_x, 1 - b, y),
        (a_y, b_y, b, 1 - y),
        (a_xy, b_xy, 1 - b, 1 - y),
    ):
        starts = row_starts(q, bb, yy)
        placed += [(starts[0], first), (starts[1], second)]
    return assemble(8 * q, placed)


def bring_home(place, own):
    q = own.shape[0] // 2
    y, b = place.y, place.b
    got = send(own, place.home_x)
    pieces = (
        (own, b, y),
        (got, 1 - b, y),
        (send(own, place.home_y), b, 1 - y),
        (send(got, place.home_y), 1 - b, 1 - y),
    )
    placed = []
    for rows, bb, yy in pieces:
        rows = jnp.where(place.keeper, rows, send(rows, place.home_core))
        starts = row_starts(q, bb, yy)
        placed += [(starts[0], rows[:q]), (starts[1], rows[q:])]
    return assemble(8 * q, placed)


def decay_block(start, row_segment, col_segment, decay):
    shape = (row_segment.shape[0], col_segment.shape[1])
    gap = lax.broadcasted_iota(jnp.int32, shape, 0) - lax.broadcasted_iota(jnp.int32, shape, 1)
    gap = gap + start
    keep = (gap >= 0) & (row_segment == col_segment)
    distance = jnp.maximum(gap, 0).astype(jnp.float32)
    return jnp.where(keep, jnp.exp(distance * decay), 0.0)


def forward_kernel(head, na, given, *refs):
    log_gamma, row_segment, col_segment, cosine, sine, growth, tokens = refs[:7]
    pieces = refs[7 : 7 + 2 * na]
    full, parts, normed, scale, sems = refs[7 + 2 * na + given :]
    width = full.shape[0] // (2 * na)
    a, c = lax.axis_index("dp") // 2, lax.axis_index("tensor") % 2
    copies = []
    for j in range(na):
        for side in range(2):
            at = 2 * lax.rem(a - j + na, na) + (c if side == 0 else 1 - c)
            at = pl.ds(pl.multiple_of(at * width, width), width)
            piece = pieces[j + side * na].at[pl.ds(0, width), :]
            copies.append(pltpu.make_async_copy(piece, full.at[at, :], sems.at[2 * j + side]))
            copies[-1].start()
    for copy in copies:
        copy.wait()
    length = tokens.shape[0]
    rows = min(512, length)
    half = HEAD_KEY // 2

    def project(r, carry):
        at = pl.ds(pl.multiple_of(r * rows, rows), rows)
        left = tokens[at, :]
        for start in range(0, HEAD_VALUE, 256):
            stop = start + 256
            parts[at, start:stop] = dot_nn(left, full[:, start:stop]).astype(jnp.bfloat16)
        cos, sin, grow = cosine[at, :], sine[at, :], growth[at, :]
        for start, factor in (
            (HEAD_VALUE, grow),
            (HEAD_VALUE + HEAD_KEY, (1.0 / grow)),
        ):
            last = 1.0 if start == HEAD_VALUE else HEAD_KEY ** (-0.5)
            part = dot_nn(left, full[:, start : start + HEAD_KEY])
            first, second = part[:, :half], part[:, half:]
            parts[at, start : start + half] = (
                (first * cos - second * sin) * factor * last
            ).astype(jnp.bfloat16)
            parts[at, start + half : start + HEAD_KEY] = (
                (second * cos + first * sin) * factor * last
            ).astype(jnp.bfloat16)
        return carry

    lax.fori_loop(0, length // rows, project, 0)
    decay = log_gamma[head]
    query = slice(HEAD_VALUE, HEAD_VALUE + HEAD_KEY)
    key = slice(HEAD_VALUE + HEAD_KEY, HEAD_VALUE + 2 * HEAD_KEY)
    for i in range(length // rows):
        to = slice(i * rows, (i + 1) * rows)
        mixed = None
        for j in range(i + 1):
            of = slice(j * rows, (j + 1) * rows)
            mask = decay_block((i - j) * rows, row_segment[to, :], col_segment[:, of], decay)
            weighted = (dot_nt(parts[to, query], parts[of, key]) * mask).astype(jnp.bfloat16)
            part = dot_nn(weighted, parts[of, :HEAD_VALUE])
            mixed = part if mixed is None else mixed + part
        unit, inverse = norm_parts(mixed, GROUP_EPSILON)
        normed[to, :] = unit
        scale[to, :] = inverse


def retention_forward(place, head, shared, pieces, held):
    log_gamma, row_segment, col_segment, *tables, tokens = shared
    length, depth = tokens.shape
    heads = log_gamma.shape[0]
    width = HEAD_VALUE + 2 * HEAD_KEY
    anywhere = pl.BlockSpec(memory_space=pl.ANY)
    whole = lambda item: pl.BlockSpec(item.shape, lambda i: (0, 0))
    return pl.pallas_call(
        functools.partial(forward_kernel, head, place.na, len(held)),
        grid=(1,),
        in_specs=[
            pl.BlockSpec(memory_space=pltpu.SMEM),
            *[whole(item) for item in shared[1:]],
            *[anywhere] * (len(pieces) + len(held)),
        ],
        out_specs=[
            pl.BlockSpec((depth, width), lambda i: (0, 0)),
            pl.BlockSpec((length, width), lambda i: (0, head)),
            pl.BlockSpec((length, HEAD_VALUE), lambda i: (0, head)),
            pl.BlockSpec((None, length, 1), lambda i: (head, 0, 0)),
        ],
        out_shape=[
            jax.ShapeDtypeStruct((depth, width), jnp.bfloat16),
            jax.ShapeDtypeStruct((length, heads * width), jnp.bfloat16),
            jax.ShapeDtypeStruct((length, heads * HEAD_VALUE), jnp.float32),
            jax.ShapeDtypeStruct((heads, length, 1), jnp.float32),
        ],
        scratch_shapes=[pltpu.SemaphoreType.DMA((len(pieces),))],
        input_output_aliases={7 + len(pieces) + i: 1 + i for i in range(len(held))},
        compiler_params=pltpu.CompilerParams(vmem_limit_bytes=56 << 20),
        cost_estimate=pl.CostEstimate(
            flops=2 * length * (depth * width + length * (HEAD_KEY + HEAD_VALUE)),
            bytes_accessed=4 * length * width + 8 * depth * width,
            transcendentals=length * length,
        ),
    )(log_gamma, row_segment, col_segment, *tables, tokens, *pieces, *held)


def retention_kernel(
    log_gamma,
    row_segment,
    col_segment,
    cosine,
    sine,
    growth,
    value,
    query,
    key,
    grad,
    normed,
    scale,
    out,
    mixed,
    grad_query,
    grad_key,
    grad_value,
):
    length = query.shape[0]
    rows = min(512, length)
    decay = log_gamma[pl.program_id(0)]
    grads, unit = grad[...], normed[...]
    mixed[...] = (
        scale[...]
        * (
            grads
            - jnp.mean(grads, axis=-1, keepdims=True)
            - unit * jnp.mean(grads * unit, axis=-1, keepdims=True)
        )
    ).astype(jnp.bfloat16)
    for i in range(length // rows):
        to = slice(i * rows, (i + 1) * rows)
        for j in range(i + 1):
            of = slice(j * rows, (j + 1) * rows)
            mask = decay_block((i - j) * rows, row_segment[to, :], col_segment[:, of], decay)
            weighted = (dot_nt(query[to, :], key[of, :]) * mask).astype(jnp.bfloat16)
            raw = (dot_nt(mixed[to, :], value[of, :]) * mask).astype(jnp.bfloat16)
            parts = (
                (grad_query, to, dot_nn(raw, key[of, :]), j == 0),
                (grad_key, of, dot_tn(raw, query[to, :]), i == j),
                (grad_value, of, dot_tn(weighted, mixed[to, :]), i == j),
            )
            for total, at, part, first in parts:
                if first:
                    total[at, :] = part
                else:
                    total[at, :] += part
    cos, sin, grow = cosine[...], sine[...], growth[...]
    out[:, :HEAD_VALUE] = grad_value[...].astype(jnp.bfloat16)
    half = HEAD_KEY // 2
    for start, total, factor, last in (
        (HEAD_VALUE, grad_query, grow, 1.0),
        (HEAD_VALUE + HEAD_KEY, grad_key, 1.0 / grow, HEAD_KEY ** (-0.5)),
    ):
        first, second = total[:, :half] * factor, total[:, half:] * factor
        out[:, start : start + half] = ((first * cos + second * sin) * last).astype(jnp.bfloat16)
        out[:, start + half : start + HEAD_KEY] = ((second * cos - first * sin) * last).astype(
            jnp.bfloat16
        )


def retention_backward(
    log_gamma, row_segment, col_segment, cosine, sine, growth, vqk, grad, normed, scale
):
    length = vqk.shape[0]
    heads = log_gamma.shape[0]
    whole = lambda item: pl.BlockSpec(item.shape, lambda h: (0, 0))
    width = HEAD_VALUE + 2 * HEAD_KEY
    each, skip = width // HEAD_KEY, HEAD_VALUE // HEAD_KEY
    shared = (row_segment, col_segment, cosine, sine, growth)
    return pl.pallas_call(
        retention_kernel,
        grid=(heads,),
        in_specs=[
            pl.BlockSpec(memory_space=pltpu.SMEM),
            *[whole(item) for item in shared],
            pl.BlockSpec((length, HEAD_VALUE), lambda h: (0, h * (width // HEAD_VALUE))),
            pl.BlockSpec((length, HEAD_KEY), lambda h: (0, h * each + skip)),
            pl.BlockSpec((length, HEAD_KEY), lambda h: (0, h * each + skip + 1)),
            pl.BlockSpec((length, HEAD_VALUE), lambda h: (0, h)),
            pl.BlockSpec((length, HEAD_VALUE), lambda h: (0, h)),
            pl.BlockSpec((None, length, 1), lambda h: (h, 0, 0)),
        ],
        out_specs=pl.BlockSpec((length, width), lambda h: (0, h)),
        out_shape=jax.ShapeDtypeStruct((length, heads * width), jnp.bfloat16),
        scratch_shapes=[
            pltpu.VMEM((length, HEAD_VALUE), jnp.bfloat16),
            pltpu.VMEM((length, HEAD_KEY), jnp.float32),
            pltpu.VMEM((length, HEAD_KEY), jnp.float32),
            pltpu.VMEM((length, HEAD_VALUE), jnp.float32),
        ],
        compiler_params=pltpu.CompilerParams(vmem_limit_bytes=48 << 20),
        cost_estimate=pl.CostEstimate(
            flops=heads * length * length * 2 * (2 * HEAD_VALUE + 3 * HEAD_KEY),
            bytes_accessed=heads * length * (4 * width + 8 * HEAD_VALUE),
            transcendentals=heads * length * length,
        ),
    )(log_gamma, *shared, vqk, vqk, vqk, grad, normed, scale)


def local(ndp, nt, *args):
    return layer(ndp, nt, *args)


def layer(
    ndp,
    nt,
    tokens,
    w_query,
    w_key,
    w_value,
    w_gate,
    w_out,
    w_ffgate,
    w_ffup,
    w_down,
    norm1_gain,
    norm1_shift,
    norm2_gain,
    norm2_shift,
    segment_ids,
    decay_index,
    cotangent,
):
    place = Place(ndp, nt)
    heads = w_query.shape[1] // HEAD_KEY
    inner = heads * HEAD_VALUE
    units = w_ffgate.shape[1]

    width = norm1_gain.shape[0]
    norms = jnp.concatenate([norm1_gain, norm1_shift, norm2_gain, norm2_shift])
    across = w_value.shape[1]
    extra = -(-norms.shape[0] // across)
    norms = jnp.pad(norms, (0, 16 * across - norms.shape[0])).reshape(16, across)
    shards = [
        jnp.concatenate(
            [
                w_value[:, h * HEAD_VALUE : (h + 1) * HEAD_VALUE],
                w_query[:, h * HEAD_KEY : (h + 1) * HEAD_KEY],
                w_key[:, h * HEAD_KEY : (h + 1) * HEAD_KEY],
            ],
            axis=1,
        )
        for h in range(heads)
    ]
    own_value = my_sequence(place, jnp.concatenate([shards[0], norms], axis=0))
    own_qk = my_sequence(place, shards[1])
    shard_og = jnp.concatenate([w_out.T, w_gate], axis=1)
    shard_ff = jnp.concatenate([w_ffgate, w_ffup], axis=1)
    shard_down = w_down.T
    got_tokens = send(tokens, place.swap)
    got_og = send(shard_og, place.swap)
    got_ff = send(shard_ff, place.swap)
    got_down = send(shard_down, place.swap)
    got_cotangent = send(cotangent, place.swap)
    value_pieces, qk_pieces = [own_value], [own_qk]
    for _ in range(1, place.na):
        value_pieces.append(send(value_pieces[-1], place.ring))
        qk_pieces.append(send(qk_pieces[-1], place.ring))
    value_others = [send(piece, place.core) for piece in value_pieces]
    qk_others = [send(piece, place.core) for piece in qk_pieces]
    norms = jnp.zeros((place.ndp, 4 * width), norms.dtype)
    for j in range(place.na):
        for piece, c in ((value_pieces[j], place.c), (value_others[j], 1 - place.c)):
            row = piece[width : width + extra].reshape(1, extra * across)[:, : 4 * width]
            at = 2 * ((place.a - j) % place.na) + c
            norms = lax.dynamic_update_slice_in_dim(norms, row, at, axis=0)
    norms = norms.reshape(place.ndp, 4, width).transpose(1, 0, 2).reshape(4, place.ndp * width)
    norms = norms.astype(jnp.float32)
    gain_one, shift_one, gain_two, shift_two = norms[0], norms[1], norms[2], norms[3]
    got_og, value_pieces[-2] = together(got_og, value_pieces[-2])
    got_tokens, qk_pieces[-2] = together(got_tokens, qk_pieces[-2])
    own_og = pick(place.keeper, shard_og, got_og)
    inputs = pick(place.keeper, tokens, got_tokens)
    full_og = queue_gather(place, own_og)
    full_out, full_gate = full_og[:, :inner], full_og[:, inner:]
    segment = my_sequence(place, segment_ids)
    decay = jnp.where(place.keeper, decay_index, send(decay_index, place.core))
    log_gamma = jnp.log1p(-jnp.exp2(-5.0 - decay.astype(jnp.float32)))

    normed_all, _ = norm_parts(inputs.astype(jnp.float32), EPSILON)
    first_in = (normed_all * gain_one + shift_one).astype(jnp.bfloat16)
    tables = xpos_tables(LENGTH, HEAD_KEY)
    shared = (log_gamma, segment[:, None], segment[None, :], *tables, first_in)
    full_value, *held = retention_forward(place, 0, shared, value_pieces + value_others, ())
    full_qk, *held = retention_forward(place, 1, shared, qk_pieces + qk_others, held)
    vqk_rot, grouped_flat, group_scale = held
    got_ff, got_down, full_value = together(got_ff, got_down, full_value)
    full_ff = queue_gather(place, pick(place.keeper, shard_ff, got_ff))
    full_down = queue_gather(place, pick(place.keeper, shard_down, got_down))
    gate = dot_nn(first_in, full_gate)
    sigmoid_gate = jax.nn.sigmoid(gate)
    swish = gate * sigmoid_gate
    gated = (swish * grouped_flat).astype(jnp.bfloat16)
    got_cotangent, gated = together(got_cotangent, gated)
    grad_feed = pick(place.keeper, cotangent, got_cotangent)

    own_inputs = my_rows(place, inputs).astype(jnp.float32)
    away = dot_nt(far_rows(place, gated), full_out).astype(jnp.bfloat16)
    got = send_far(place, away)
    here = dot_nt(near_rows(place, after(gated, away)), full_out)
    middle = own_inputs + sum_near(place, here, got)
    normed_two, scale_two = norm_parts(middle, EPSILON)
    second_in = gather_rows(place, (normed_two * gain_two + shift_two).astype(jnp.bfloat16))

    ff_both = dot_nn(second_in, full_ff)
    ff_gate, ff_up = ff_both[:, :units], ff_both[:, units:]
    hidden = (ff_gate * (0.5 * (1.0 + lax.erf(ff_gate * INV_ROOT2))) * ff_up).astype(jnp.bfloat16)
    hidden, ff_both = together(hidden, ff_both)
    feed_near, feed_far = core_halves(place, grad_feed)
    down_got, _ = core_far(place, feed_far, hidden)
    down_sum = core_near(feed_near, hidden, down_got)
    down_sum, full_down = together(down_sum, full_down)
    share_down = queue_scatter(place, down_sum)
    ff_gate, ff_up = ff_both[:, :units], ff_both[:, units:]
    normal_cdf = 0.5 * (1.0 + lax.erf(ff_gate * INV_ROOT2))
    activation = ff_gate * normal_cdf
    e_away = dot_nt(far_rows(place, hidden), full_down).astype(jnp.bfloat16)
    grad_hidden = dot_nn(grad_feed, full_down)
    density = jnp.exp(-0.5 * ff_gate * ff_gate) * INV_ROOT_TWO_PI
    grad_ff = jnp.concatenate(
        [
            (grad_hidden * ff_up * (normal_cdf + ff_gate * density)).astype(jnp.bfloat16),
            (grad_hidden * activation).astype(jnp.bfloat16),
        ],
        axis=1,
    )
    second_near, second_far = core_halves(place, second_in)
    away = dot_nt(far_rows(place, grad_ff), full_ff).astype(jnp.bfloat16)
    got = send_far(place, away)
    ff_got, ff_far = core_far(place, second_far, after(grad_ff, away))
    here = dot_nt(near_rows(place, after(grad_ff, ff_far)), full_ff)
    ff_sum = core_near(second_near, after(grad_ff, here), ff_got)
    share_ff = queue_scatter(place, ff_sum)
    grad_second = sum_near(place, here, got)
    grad_middle = my_rows(place, grad_feed).astype(jnp.float32) + norm_back(
        grad_second, normed_two, scale_two, gain_two
    )
    grad_branch = gather_rows(place, grad_middle.astype(jnp.bfloat16))
    e_got = send_far(place, e_away)
    branch_near, branch_far = core_halves(place, grad_branch)
    first_near, first_far = core_halves(place, first_in)
    out_got, out_far = core_far(place, branch_far, gated)
    grad_gated = dot_nn(after(grad_branch, out_far), full_out)
    swish_slope = sigmoid_gate * (1.0 + gate * (1.0 - sigmoid_gate))
    grad_gate_in = (grad_gated * grouped_flat * swish_slope).astype(jnp.bfloat16)
    grad_grouped = grad_gated * swish
    gate_got, gate_far = core_far(place, first_far, grad_gate_in)
    out_sum = core_near(branch_near, after(gated, gate_far), out_got)
    gate_sum = core_near(first_near, after(grad_gate_in, out_sum), gate_got)
    og_sum = jnp.concatenate([out_sum, gate_sum], axis=1)
    grad_grouped, og_sum, e_near = together(grad_grouped, og_sum, near_rows(place, hidden))
    share_og = queue_scatter(place, og_sum)
    here = dot_nt(e_near, full_down)
    feed = sum_near(place, here, e_got)
    block_out = bring_home(place, (middle + feed).astype(jnp.bfloat16))
    grad_vqk = retention_backward(*shared[:-1], vqk_rot, grad_grouped, grouped_flat, group_scale)

    def first_product(gate_rows, vqk_rows):
        return (
            dot_nt(gate_rows, full_gate)
            + dot_nt(vqk_rows[:, :inner], full_value)
            + dot_nt(vqk_rows[:, inner:], full_qk)
        )

    vqk_got, vqk_far = core_far(place, first_far, grad_vqk)
    ready = after(grad_vqk, vqk_far)
    away = first_product(far_rows(place, grad_gate_in), far_rows(place, ready)).astype(jnp.bfloat16)
    got = send_far(place, away)
    vqk_sum = core_near(first_near, after(grad_vqk, away), vqk_got)
    ready, vqk_sum = together(grad_vqk, vqk_sum)
    share_vqk = queue_scatter(place, vqk_sum)
    here = first_product(near_rows(place, grad_gate_in), near_rows(place, ready))
    grad_first = sum_near(place, here, got)
    normed_one, scale_one = norm_parts(own_inputs, EPSILON)
    grad_tokens = grad_middle + norm_back(grad_first, normed_one, scale_one, gain_one)
    grad_tokens = bring_home(place, grad_tokens.astype(jnp.bfloat16)).astype(jnp.float32)
    vectors = vector_grads(
        place,
        jnp.stack(
            [
                jnp.sum(grad_first * normed_one, axis=0),
                jnp.sum(grad_first, axis=0),
                jnp.sum(grad_second * normed_two, axis=0),
                jnp.sum(grad_second, axis=0),
            ]
        ),
    )
    share_down = to_owner(place, share_down).T
    share_ff = to_owner(place, share_ff)
    share_og = to_owner(place, share_og)
    share_vqk, grad_tokens = together(share_vqk, grad_tokens)
    share_vqk = to_owner(place, share_vqk)
    picks = []
    for start, size in ((HEAD_VALUE, HEAD_KEY), (HEAD_VALUE + HEAD_KEY, HEAD_KEY), (0, HEAD_VALUE)):
        each = HEAD_VALUE + 2 * HEAD_KEY
        picks.append(
            jnp.concatenate(
                [share_vqk[:, h * each + start : h * each + start + size] for h in range(heads)], axis=1
            )
        )
    return (
        block_out,
        grad_tokens,
        *picks,
        share_og[:, inner:],
        share_og[:, :inner].T,
        share_ff[:, :units],
        share_ff[:, units:],
        share_down,
        vectors[0],
        vectors[1],
        vectors[2],
        vectors[3],
    )


def solution(mesh):
    placed = (
        P("dp", None),
        P("dp", "tensor"),
        P("dp", "tensor"),
        P("dp", "tensor"),
        P("dp", "tensor"),
        P("tensor", "dp"),
        P("dp", "tensor"),
        P("dp", "tensor"),
        P("tensor", "dp"),
        P("dp"),
        P("dp"),
        P("dp"),
        P("dp"),
        P("dp"),
        P("tensor"),
        P("dp", None),
    )
    return jax.shard_map(
        functools.partial(local, mesh.shape["dp"], mesh.shape["tensor"]),
        mesh=mesh,
        in_specs=placed,
        out_specs=(
            P("dp", None),
            P("dp", None),
            P("dp", "tensor"),
            P("dp", "tensor"),
            P("dp", "tensor"),
            P("dp", "tensor"),
            P("tensor", "dp"),
            P("dp", "tensor"),
            P("dp", "tensor"),
            P("tensor", "dp"),
            P("dp"),
            P("dp"),
            P("dp"),
            P("dp"),
        ),
        check_vma=False,
    )
```
